512 devices in a mesh: row: 16 (over y, x_hi), col: 32 (over z, x_lo, core).
Axes of the slice: x: 4 (x_hi: 2, x_lo: 2; x = x_hi * 2 + x_lo), y: 8, z: 8, core: 2. Of those that a mesh axis runs over, the one named last changes fastest.
Arguments:
- features: bfloat16 [32, 2048, 128], P('col'), may hold values from -6 to 6
- dst_features: bfloat16 [65536, 128], P(('row', 'col')), may hold values from -6 to 6
- w_self: bfloat16 [128, 256], replicated, may hold values from -0.5 to 0.5
- w_neigh: bfloat16 [128, 256], replicated, may hold values from -0.5 to 0.5
- cotangent: bfloat16 [65536, 256], P(('row', 'col')), may hold values from -6 to 6
- block_values: bfloat16 [16, 32, 32, 128, 128], P('row', 'col'), may hold values from -0.15625 to 0.15625
- block_rows: int32 [16, 32, 32], P('row', 'col'), may hold values from 0 to 31, as said below
- block_cols: int32 [16, 32, 32], P('row', 'col'), may hold values from 0 to 15
- block_counts: int32 [16, 32], P('row', 'col'), may hold values from 4 to 32, as said below
Outputs:
- output: bfloat16 [65536, 256], P(('row', 'col'))
- grad_w_self: float32 [128, 256], replicated
- grad_w_neigh: float32 [128, 256], replicated
- grad_features: float32 [32, 2048, 128], P('col', 'row')
The draws below stay inside these ranges and needn't reach their ends.
Inputs may be any that keep to these rules, and one draw needn't show every extreme that they name: On one device the slots name distinct pairs of block_rows and block_cols, also in unused slots. `block_counts`: some device uses all 32 slots in every draw.
All inputs are finite; a program needn't handle non-finite values.
Results may differ from the reference program's by a relative error of at most 0.0052.
Values may be sent and summed in bfloat16 or wider, within the bound.
A program may use at most 64 MiB of HBM per device.

```python
import math
import jax
import jax.numpy as jnp
from jax import lax

F = 128
H = 256
BLOCK = 128
DST_DEV = 128
CB = 16
SLOTS = 32
RB = 32
DST = 65536
N_ROW = 16
N_COL = 32


def slot_table(key):
    base_key = jax.random.fold_in(key, 7)
    device_keys = jax.random.split(base_key, N_ROW * N_COL)

    def one_device(device_key):
        return jax.random.permutation(device_key, RB * CB)[:SLOTS]
    chosen = jax.vmap(one_device)(device_keys)
    return chosen.reshape(N_ROW, N_COL, SLOTS).astype(jnp.int32)


def draw_block_rows(key, part):
    return slot_table(key) // CB


def draw_block_cols(key, part):
    return slot_table(key) % CB


def draw_block_counts(key, part):
    base_key = jax.random.fold_in(key, 11)
    first_key, second_key, third_key = jax.random.split(base_key, 3)
    first_draw = jax.random.randint(first_key, (N_ROW, N_COL), 0, SLOTS + 1)
    second_draw = jax.random.randint(second_key, (N_ROW, N_COL), 0, SLOTS + 1)
    counts_all = jnp.maximum(first_draw * second_draw // SLOTS, SLOTS // 8)
    busiest = jax.random.randint(third_key, (), 0, N_ROW * N_COL)
    counts_all = counts_all.reshape(-1).at[busiest].set(SLOTS)
    return counts_all.reshape(N_ROW, N_COL).astype(jnp.int32)


def steps_of(key, extent, shards, low, top_value):
    gain = 1.0
    for axis_at, blocks in shards:
        steps = jax.random.uniform(jax.random.fold_in(jax.random.fold_in(key, 6), axis_at), (blocks,), jnp.float32, low / len(shards), top_value / len(shards))
        gain = gain * jnp.repeat(jnp.exp(steps), extent[axis_at] // blocks).reshape((-1,) + (1,) * (len(extent) - 1 - axis_at))
    return gain


def bell_draw(stream_key, shape, deviation, bound, cuts=(), kind=jnp.bfloat16):
    values = deviation * jax.random.normal(stream_key, shape, jnp.float32)
    if cuts:
        values = values * steps_of(stream_key, shape, cuts, -0.22, 0.18)
    return jnp.clip(values, -bound, bound).astype(kind)


def setup_inputs(seed: int = 0) -> dict:
    arg_keys = jax.random.split(jax.random.key(seed), 10)
    return {
        "features": bell_draw(arg_keys[0], (N_COL, CB * BLOCK, F), 1.0, 6.0, ((0, 32),)),
        "dst_features": bell_draw(arg_keys[1], (DST, F), 1.0, 6.0, ((0, 512),)),
        "w_self": bell_draw(arg_keys[2], (F, H), F ** -0.5, 0.5),
        "w_neigh": bell_draw(arg_keys[3], (F, H), F ** -0.5, 0.5),
        "cotangent": bell_draw(arg_keys[4], (DST, H), 1.0, 6.0, ((0, 512),)),
        "block_values": bell_draw(arg_keys[5], (N_ROW, N_COL, SLOTS, BLOCK, BLOCK), (3 * BLOCK * BLOCK * SLOTS // (10 * DST_DEV)) ** -0.5, 0.15625, ((0, 16), (1, 32))),
        "block_rows": draw_block_rows(jax.random.fold_in(arg_keys[9], 71), 0),
        "block_cols": draw_block_cols(jax.random.fold_in(arg_keys[9], 71), 0),
        "block_counts": draw_block_counts(jax.random.fold_in(arg_keys[9], 71), 0),
    }


def reference(features, dst_features, w_self, w_neigh, cotangent, block_values, block_rows, block_cols, block_counts):
    source_blocks = features.reshape(N_COL, CB, BLOCK, F)
    col_index = jnp.arange(N_COL, dtype=jnp.int32)[:, None]
    slot_index = jnp.arange(SLOTS, dtype=jnp.int32)[None, :]

    def slab_forward(group_args):
        slab_vals, slab_rows, slab_cols, slab_counts = group_args
        live_mask = (slot_index < slab_counts[:, None]).astype(jnp.float32)
        picked = source_blocks[col_index, slab_cols].astype(jnp.float32)
        products = jnp.einsum('csij,csjf->csif', slab_vals.astype(jnp.float32), picked, precision=lax.Precision.HIGHEST)
        products = products * live_mask[:, :, None, None]
        summed = jax.ops.segment_sum(products.reshape(N_COL * SLOTS, BLOCK, F), slab_rows.reshape(-1).astype(jnp.int32), num_segments=RB)
        return summed.reshape(RB * BLOCK, F)
    aggregate = lax.map(slab_forward, (block_values, block_rows, block_cols, block_counts))
    aggregate = aggregate.reshape(DST, F).astype(jnp.bfloat16)
    pre_act = jnp.dot(dst_features, w_self, preferred_element_type=jnp.float32) + jnp.dot(aggregate, w_neigh, preferred_element_type=jnp.float32)
    sigmoid_pre = jax.nn.sigmoid(pre_act)
    output = (pre_act * sigmoid_pre).astype(jnp.bfloat16)
    grad_pre = (cotangent.astype(jnp.float32) * sigmoid_pre * (1.0 + pre_act * (1.0 - sigmoid_pre))).astype(jnp.bfloat16)
    scale_factor = 1.0 / math.sqrt(DST)
    grad_w_self = jnp.dot(dst_features.T, grad_pre, preferred_element_type=jnp.float32) * scale_factor
    grad_w_neigh = jnp.dot(aggregate.T, grad_pre, preferred_element_type=jnp.float32) * scale_factor
    slab_grads = jnp.dot(grad_pre, w_neigh.T, preferred_element_type=jnp.float32).astype(jnp.bfloat16)
    slab_grads = slab_grads.reshape(N_ROW, RB, BLOCK, F)

    def slab_backward(running, group_args):
        slab_grad, slab_vals, slab_rows, slab_cols, slab_counts = group_args
        live_mask = (slot_index < slab_counts[:, None]).astype(jnp.float32)
        picked = slab_grad[slab_rows].astype(jnp.float32)
        products = jnp.einsum('csij,csif->csjf', slab_vals.astype(jnp.float32), picked, precision=lax.Precision.HIGHEST)
        products = products * live_mask[:, :, None, None]
        targets = (col_index * CB + slab_cols).reshape(-1).astype(jnp.int32)
        added = jax.ops.segment_sum(products.reshape(N_COL * SLOTS, BLOCK, F), targets, num_segments=N_COL * CB)
        return (running + added, None)
    zero_grads = jnp.zeros((N_COL * CB, BLOCK, F), jnp.float32)
    source_grad, unused = lax.scan(slab_backward, zero_grads, (slab_grads, block_values, block_rows, block_cols, block_counts))
    return (output, grad_w_self, grad_w_neigh, source_grad.reshape(N_COL, CB * BLOCK, F))
```

```python
import functools
import math

import jax
import jax.numpy as jnp
from jax import lax
from jax.experimental import pallas as pl
from jax.experimental.pallas import tpu as pltpu
from jax.sharding import PartitionSpec as P

BF16 = jnp.bfloat16
F32 = jnp.float32
MESH = pl.DeviceIdType.MESH
N = 8
VMEM = pl.BlockSpec(memory_space=pltpu.VMEM)
SMEM = pl.BlockSpec(memory_space=pltpu.SMEM)
LIMIT = 32 * 1024 * 1024


def near(i):
    hop = i // 2 + 1
    return hop + (i % 2) * (N - 2 * hop)


def far(i):
    return near(N - 2 - i)


def loop(n, body):
    lax.fori_loop(0, n, lambda i, c: (body(i), c)[1], 0)


def remote(src, dst, send, recv, device):
    return pltpu.make_async_remote_copy(
        src_ref=src, dst_ref=dst, send_sem=send, recv_sem=recv, device_id=device, device_id_type=MESH
    )


def col_parts():
    c = lax.axis_index("col")
    return c // 4, (c // 2) % 2, c % 2


def row_parts():
    r = lax.axis_index("row")
    return r // 2, r % 2


def forward_kernel(rows, cols, counts, feats, vals, send, keep, acc):
    core = lax.axis_index("col") % 2
    slots = vals.shape[0]
    live = counts[0, 0]
    half = keep.shape[0]
    acc[...] = jnp.zeros_like(acc)
    for s in range(slots):
        r = rows[0, 0, s]
        at = ((r + core) % 2) * half + ((r // 2) % 2) * N + r // 4
        at = jnp.where(s < live, at, 2 * half)
        acc[at] += jnp.dot(vals[s], feats[cols[0, 0, s]], preferred_element_type=F32)
    keep[...] = acc[:half]
    send[...] = acc[half : 2 * half].astype(BF16)


def backward_kernel(rows, cols, counts, grads, vals, send, keep, acc):
    side = lax.axis_index("row") % 2
    slots = vals.shape[0]
    live = counts[0, 0]
    half = keep.shape[0]
    acc[...] = jnp.zeros_like(acc)
    for s in range(slots):
        r = rows[0, 0, s]
        c = cols[0, 0, s]
        at = ((c + side) % 2) * half + c // 2
        at = jnp.where(s < live, at, 2 * half)
        g = grads[(r % 2) * 16 + ((r // 2) % 2) * N + r // 4]
        acc[at] += lax.dot_general(vals[s], g, (((0,), (0,)), ((), ())), preferred_element_type=F32)
    keep[...] = acc[:half]
    send[...] = acc[half : 2 * half].astype(BF16)


def products(kernel, half, rows, cols, counts, table, vals):
    block, width = vals.shape[-1], table.shape[-1]
    slots = vals.shape[0]
    return pl.pallas_call(
        kernel,
        out_shape=(
            jax.ShapeDtypeStruct((half, block, width), BF16),
            jax.ShapeDtypeStruct((half, block, width), F32),
        ),
        in_specs=[SMEM, SMEM, SMEM, VMEM, VMEM],
        out_specs=(VMEM, VMEM),
        scratch_shapes=[pltpu.VMEM((2 * half + 1, block, width), F32)],
        compiler_params=pltpu.CompilerParams(vmem_limit_bytes=LIMIT),
        cost_estimate=pl.CostEstimate(
            flops=2 * slots * block * block * width,
            bytes_accessed=2 * slots * block * block + 6 * half * block * width,
            transcendentals=0,
        ),
    )(rows, cols, counts, table, vals)


def dense_kernel(
    psend, pkeep, dst, cot, w_self, w_neigh,
    out, grads, wpart,
    got_c, x_send, got_x, z_send, got_z, own,
    w_full, w_c, w_xs, w_x, w_zs, w_z,
    c_s, c_r, x_s, x_r, z_s, z_r,
    gz_s, gz_r, gx_s, gx_r, gc_s, gc_r,
    wc_s, wc_r, wx_s, wx_r, wz_s, wz_r,
):
    row = lax.axis_index("row")
    z, x, k = col_parts()
    sibling = (row, z * 4 + x * 2 + (1 - k))
    beside = (row, z * 4 + (1 - x) * 2 + k)

    def ring(d):
        other = (z + d) % N
        return other, (row, other * 4 + x * 2 + k)

    barrier = pltpu.get_barrier_semaphore()
    pl.semaphore_signal(barrier, inc=1, device_id=sibling, device_id_type=MESH)
    pl.semaphore_signal(barrier, inc=1, device_id=beside, device_id_type=MESH)
    for d in range(1, N):
        pl.semaphore_signal(barrier, inc=1, device_id=ring(d)[1], device_id_type=MESH)
    pl.semaphore_wait(barrier, N + 1)

    def c_copy(at):
        return remote(psend.at[at], got_c.at[at], c_s.at[at], c_r.at[at], sibling)

    away, here = (1 - x) * N, x * N

    def c_start(i):
        c_copy(away + (z + far(i)) % N).start()

    def c_start_here(i):
        c_copy(here + (z + far(i)) % N).start()

    loop(N - 1, c_start)
    c_copy(away + z).start()
    loop(N - 1, c_start_here)
    c_copy(here + z).start()

    def x_copy(at):
        return remote(x_send.at[at], got_x.at[at], x_s.at[at], x_r.at[at], beside)

    def x_step(at):
        c_copy(away + at).wait_recv()
        x_send[at] = (pkeep[away + at] + got_c[away + at].astype(F32)).astype(BF16)
        x_copy(at).start()

    loop(N - 1, lambda i: x_step((z + far(i)) % N))
    x_step(z)

    pre_self = jnp.dot(dst[...], w_self[...], preferred_element_type=F32)

    def z_copy(d):
        other, device = ring(d)
        return remote(z_send.at[other], got_z.at[z], z_s.at[d], z_r.at[d], device)

    def merged(at):
        c_copy(here + at).wait_recv()
        x_copy(at).wait_recv()
        return pkeep[here + at] + got_c[here + at].astype(F32) + got_x[at].astype(F32)

    def z_step(i):
        d = far(i)
        other = (z + d) % N
        z_send[other] = merged(other).astype(BF16)
        z_copy(d).start()

    loop(N - 1, z_step)
    own[...] = merged(z)

    def z_take(i):
        d = near(i)
        z_copy(d).wait_recv()
        own[...] += got_z[(z + N - d) % N].astype(F32)

    loop(N - 1, z_take)
    agg = own[...].astype(BF16)

    pre = pre_self + jnp.dot(agg, w_neigh[...], preferred_element_type=F32)
    sig = jax.nn.sigmoid(pre)
    out[...] = (pre * sig).astype(BF16)
    gpre = (cot[...].astype(F32) * sig * (1.0 + pre * (1.0 - sig))).astype(BF16)
    me = k * 16 + x * N + z
    grads[me] = lax.dot_general(
        gpre, w_neigh[...], (((1,), (1,)), ((), ())), preferred_element_type=F32
    ).astype(BF16)

    mine = k * 16 + x * N
    besides = k * 16 + (1 - x) * N

    def gz_copy(d):
        return remote(grads.at[me], grads.at[me], gz_s.at[d], gz_r.at[d], ring(d)[1])

    def gx_copy(at):
        return remote(grads.at[mine + at], grads.at[mine + at], gx_s.at[at], gx_r.at[at], beside)

    def gc_copy(part, at):
        slot = k * 16 + part * N + at
        sem = part * N + at
        return remote(grads.at[slot], grads.at[slot], gc_s.at[sem], gc_r.at[sem], sibling)

    loop(N - 1, lambda i: gz_copy(far(i)).start())
    gx_copy(z).start()
    gc_copy(x, z).start()

    feat = dst.shape[1]
    pieces, tall, hid = w_full.shape
    for base, left in ((0, dst[...]), (1, agg)):
        dw = lax.dot_general(left, gpre, (((0,), (0,)), ((), ())), preferred_element_type=F32)
        w_full[pl.ds(base * (feat // tall), feat // tall)] = dw.reshape(feat // tall, tall, hid)
    half = pieces // 2
    wc_copy = remote(w_full.at[pl.ds((1 - k) * half, half)], w_c, wc_s, wc_r, sibling)
    wc_copy.start()

    def forward(i):
        d = near(i)
        other = (z + N - d) % N
        gz_copy(d).wait_recv()
        gx_copy(other).start()
        gc_copy(x, other).start()

    lax.fori_loop(0, 2, lambda i, c: (forward(i), c)[1], 0)
    wc_copy.wait_recv()
    w_xs[...] = w_full[pl.ds(k * half + (1 - x) * N, N)] + w_c[pl.ds((1 - x) * N, N)]
    wx_copy = remote(w_xs, w_x, wx_s, wx_r, beside)
    wx_copy.start()
    lax.fori_loop(2, 4, lambda i, c: (forward(i), c)[1], 0)
    wx_copy.wait_recv()
    w_zs[...] = w_full[pl.ds(k * half + x * N, N)] + w_c[pl.ds(x * N, N)] + w_x[...]

    def wz_copy(d):
        other, device = ring(d)
        return remote(w_zs.at[other], w_z.at[z], wz_s.at[d], wz_r.at[d], device)

    loop(N - 1, lambda i: wz_copy(far(i)).start())
    lax.fori_loop(4, N - 1, lambda i, c: (forward(i), c)[1], 0)

    def gx_take(at):
        gx_copy(at).wait_recv()
        gc_copy(1 - x, at).start()

    gx_take(z)
    loop(N - 1, lambda i: gx_take((z + near(i)) % N))

    wpart[...] = w_zs[z]

    def wz_take(i):
        d = near(i)
        wz_copy(d).wait_recv()
        wpart[...] += w_z[(z + N - d) % N]

    loop(N - 1, wz_take)

    def gc_wait(i):
        gc_copy(i // N, i % N).wait_recv()

    loop(2 * N, gc_wait)

    loop(2 * N, lambda i: c_copy(i).wait_send())
    loop(N, lambda i: x_copy(i).wait_send())
    loop(N, lambda i: gx_copy(i).wait_send())
    loop(2 * N, lambda i: gc_copy(i // N, i % N).wait_send())

    def ring_sent(i):
        z_copy(i + 1).wait_send()
        gz_copy(i + 1).wait_send()
        wz_copy(i + 1).wait_send()

    loop(N - 1, ring_sent)
    wc_copy.wait_send()
    wx_copy.wait_send()


def dense(psend, pkeep, dst, cot, w_self, w_neigh):
    block, width = pkeep.shape[1:]
    hid = w_self.shape[1]
    tall = 2 * width // (4 * N)
    dma = pltpu.SemaphoreType.DMA
    return pl.pallas_call(
        dense_kernel,
        out_shape=(
            jax.ShapeDtypeStruct((block, hid), BF16),
            jax.ShapeDtypeStruct((4 * N, block, width), BF16),
            jax.ShapeDtypeStruct((tall, hid), F32),
        ),
        in_specs=[VMEM] * 6,
        out_specs=(VMEM,) * 3,
        scratch_shapes=[
            pltpu.VMEM((2 * N, block, width), BF16),
            pltpu.VMEM((N, block, width), BF16),
            pltpu.VMEM((N, block, width), BF16),
            pltpu.VMEM((N, block, width), BF16),
            pltpu.VMEM((N, block, width), BF16),
            pltpu.VMEM((block, width), F32),
            pltpu.VMEM((4 * N, tall, hid), F32),
            pltpu.VMEM((2 * N, tall, hid), F32),
            pltpu.VMEM((N, tall, hid), F32),
            pltpu.VMEM((N, tall, hid), F32),
            pltpu.VMEM((N, tall, hid), F32),
            pltpu.VMEM((N, tall, hid), F32),
            dma((2 * N,)), dma((2 * N,)), dma((N,)), dma((N,)), dma((N,)), dma((N,)),
            dma((N,)), dma((N,)), dma((N,)), dma((N,)), dma((2 * N,)), dma((2 * N,)),
            dma, dma, dma, dma, dma((N,)), dma((N,)),
        ],
        compiler_params=pltpu.CompilerParams(
            collective_id=0, has_side_effects=True, vmem_limit_bytes=LIMIT
        ),
    )(psend, pkeep, dst, cot, w_self, w_neigh)


def source_kernel(
    scale, qsend, qkeep, wpart,
    out, w_out,
    got_h, y_send, got_y, w_h, w_ys, w_y,
    h_s, h_r, y_s, y_r, wh_s, wh_r, wy_s, wy_r,
    gz_s, gz_r, gx_s, gx_r, gc_s, gc_r,
):
    row, col = lax.axis_index("row"), lax.axis_index("col")
    z, x, k = col_parts()
    y, h = row_parts()
    across = (y * 2 + (1 - h), col)
    sibling = (row, z * 4 + x * 2 + (1 - k))
    beside = (row, z * 4 + (1 - x) * 2 + k)

    def yring(d):
        other = (y + d) % N
        return other, (other * 2 + h, col)

    def zring(d):
        other = (z + d) % N
        return (row, other * 4 + x * 2 + k)

    barrier = pltpu.get_barrier_semaphore()
    for device in (across, sibling, beside):
        pl.semaphore_signal(barrier, inc=1, device_id=device, device_id_type=MESH)
    for d in range(1, N):
        pl.semaphore_signal(barrier, inc=1, device_id=yring(d)[1], device_id_type=MESH)
        pl.semaphore_signal(barrier, inc=1, device_id=zring(d), device_id_type=MESH)
    pl.semaphore_wait(barrier, 2 * N + 1)

    def h_copy(at):
        return remote(qsend.at[at], got_h.at[at], h_s.at[at], h_r.at[at], across)

    wh_copy = remote(wpart, w_h, wh_s, wh_r, across)
    wh_copy.start()
    loop(N - 1, lambda i: h_copy((y + far(i)) % N).start())
    h_copy(y).start()

    wh_copy.wait_recv()
    w_ys[...] = wpart[...] + w_h[...]
    w_y[y] = w_ys[...]

    def wy_copy(d):
        return remote(w_ys, w_y.at[y], wy_s.at[d], wy_r.at[d], yring(d)[1])

    loop(N - 1, lambda i: wy_copy(far(i)).start())

    def y_copy(d):
        other, device = yring(d)
        return remote(y_send.at[other], got_y.at[y], y_s.at[d], y_r.at[d], device)

    def y_step(i):
        d = far(i)
        other = (y + d) % N
        h_copy(other).wait_recv()
        y_send[other] = (qkeep[other] + got_h[other].astype(F32)).astype(BF16)
        y_copy(d).start()

    loop(N - 1, y_step)
    h_copy(y).wait_recv()
    out[...] = qkeep[y] + got_h[y].astype(F32)

    loop(N - 1, lambda i: wy_copy(near(i)).wait_recv())
    total = w_y[0]
    for i in range(1, N):
        total += w_y[i]
    me = k * 16 + x * N + z
    w_out[me] = total * scale

    mine = k * 16 + x * N

    def gz_copy(d):
        return remote(w_out.at[me], w_out.at[me], gz_s.at[d], gz_r.at[d], zring(d))

    def gx_copy(at):
        return remote(w_out.at[mine + at], w_out.at[mine + at], gx_s.at[at], gx_r.at[at], beside)

    def gc_copy(part, at):
        slot = k * 16 + part * N + at
        sem = part * N + at
        return remote(w_out.at[slot], w_out.at[slot], gc_s.at[sem], gc_r.at[sem], sibling)

    loop(N - 1, lambda i: gz_copy(far(i)).start())
    gx_copy(z).start()
    gc_copy(x, z).start()

    def y_take(i):
        d = near(i)
        y_copy(d).wait_recv()
        out[...] += got_y[(y + N - d) % N].astype(F32)

    def forward(i):
        d = near(i)
        other = (z + N - d) % N
        gz_copy(d).wait_recv()
        gx_copy(other).start()
        gc_copy(x, other).start()

    def gx_take(at):
        gx_copy(at).wait_recv()
        gc_copy(1 - x, at).start()

    loop(N - 1, forward)
    gx_take(z)
    loop(N - 1, lambda i: gx_take((z + near(i)) % N))
    loop(N - 1, y_take)
    loop(2 * N, lambda i: gc_copy(i // N, i % N).wait_recv())

    loop(N, lambda i: h_copy(i).wait_send())
    loop(N, lambda i: gx_copy(i).wait_send())
    loop(2 * N, lambda i: gc_copy(i // N, i % N).wait_send())

    def ring_sent(i):
        y_copy(i + 1).wait_send()
        gz_copy(i + 1).wait_send()
        wy_copy(i + 1).wait_send()

    loop(N - 1, ring_sent)
    wh_copy.wait_send()


def source(scale, qsend, qkeep, wpart):
    block, width = qkeep.shape[1:]
    tall, hid = wpart.shape
    dma = pltpu.SemaphoreType.DMA
    return pl.pallas_call(
        functools.partial(source_kernel, scale),
        out_shape=(
            jax.ShapeDtypeStruct((block, width), F32),
            jax.ShapeDtypeStruct((4 * N, tall, hid), F32),
        ),
        in_specs=[VMEM] * 3,
        out_specs=(VMEM,) * 2,
        scratch_shapes=[
            pltpu.VMEM((N, block, width), BF16),
            pltpu.VMEM((N, block, width), BF16),
            pltpu.VMEM((N, block, width), BF16),
            pltpu.VMEM((tall, hid), F32),
            pltpu.VMEM((tall, hid), F32),
            pltpu.VMEM((N, tall, hid), F32),
            dma((N,)), dma((N,)), dma((N,)), dma((N,)), dma, dma, dma((N,)), dma((N,)),
            dma((N,)), dma((N,)), dma((N,)), dma((N,)), dma((2 * N,)), dma((2 * N,)),
        ],
        compiler_params=pltpu.CompilerParams(
            collective_id=1, has_side_effects=True, vmem_limit_bytes=LIMIT
        ),
    )(qsend, qkeep, wpart)


def per_device(features, dst_features, w_self, w_neigh, cotangent, block_values, block_rows, block_cols, block_counts):
    block = block_values.shape[-1]
    width = features.shape[-1]
    vals = block_values[0, 0]
    table = features.reshape(-1, block, width)
    psend, pkeep = products(forward_kernel, 2 * N, block_rows, block_cols, block_counts, table, vals)
    out, grads, wpart = dense(psend, pkeep, dst_features, cotangent, w_self, w_neigh)
    qsend, qkeep = products(backward_kernel, N, block_rows, block_cols, block_counts, grads, vals)
    nodes = dst_features.shape[0] * lax.axis_size("row") * lax.axis_size("col")
    source_part, w_all = source(1.0 / math.sqrt(nodes), qsend, qkeep, wpart)
    w_all = w_all.reshape(2, width, -1)
    return out, w_all[0], w_all[1], source_part[None]


def solution(mesh):
    placed = (
        P("col", None, None),
        P(("row", "col"), None),
        P(),
        P(),
        P(("row", "col"), None),
        P("row", "col", None, None, None),
        P("row", "col", None),
        P("row", "col", None),
        P("row", "col"),
    )
    return jax.shard_map(
        per_device,
        mesh=mesh,
        in_specs=placed,
        out_specs=(P(("row", "col"), None), P(), P(), P("col", "row", None)),
        check_vma=False,
    )
```

```python
import functools
import math

import jax
import jax.numpy as jnp
from jax import lax
from jax.experimental import pallas as pl
from jax.experimental.pallas import tpu as pltpu
from jax.sharding import PartitionSpec as P

BF16 = jnp.bfloat16
F32 = jnp.float32
MESH = pl.DeviceIdType.MESH
N = 8
OFFSETS = (4, 3, 5, 2, 6, 1, 7, 0)
VMEM = pl.BlockSpec(memory_space=pltpu.VMEM)
SMEM = pl.BlockSpec(memory_space=pltpu.SMEM)
HBM = pl.BlockSpec(memory_space=pltpu.HBM)
DMA = pltpu.SemaphoreType.DMA


def remote(src, dst, send, recv, device):
    return pltpu.make_async_remote_copy(
        src_ref=src, dst_ref=dst, send_sem=send, recv_sem=recv, device_id=device, device_id_type=MESH
    )


def chain_kernel(rows, cols, counts, row_prev, row_last, col_prev, col_last):
    slots = row_prev.shape[0]
    live = counts[0, 0]
    for last in (row_last, col_last):
        for b in range(last.shape[0]):
            last[b] = slots
    for s in range(slots):
        for ids, prev, last in ((rows, row_prev, row_last), (cols, col_prev, col_last)):
            b = ids[0, 0, s]
            before = last[b]
            prev[s] = before
            last[b] = jnp.where(s < live, s, before)


def chains(rows, cols, counts, row_blocks, col_blocks):
    slots = rows.shape[-1]
    return pl.pallas_call(
        chain_kernel,
        out_shape=tuple(jax.ShapeDtypeStruct((n,), jnp.int32) for n in (slots, row_blocks, slots, col_blocks)),
        in_specs=[SMEM] * 3,
        out_specs=(SMEM,) * 4,
    )(rows, cols, counts)


def ring_reduce(piece, ahead, behind, sent, got_a, got_b, a_s, a_r, b_s, b_r):
    tall = sent.shape[1] // 2
    top, low = pl.ds(0, tall), pl.ds(tall, tall)

    def a_copy(hop):
        if hop == 0:
            return remote(sent.at[0, top], got_a.at[0, top], a_s.at[0], a_r.at[0], ahead)
        return remote(sent.at[2 * hop - 1], got_a.at[hop], a_s.at[hop], a_r.at[hop], ahead)

    def b_copy(hop):
        if hop == 0:
            return remote(sent.at[0, low], got_b.at[0, low], b_s.at[0], b_r.at[0], behind)
        return remote(sent.at[2 * hop], got_b.at[hop], b_s.at[hop], b_r.at[hop], behind)

    sent[0] = piece(0).astype(BF16)
    a_copy(0).start()
    b_copy(0).start()
    part = piece(1)
    sent[1, low] = part[tall:].astype(BF16)
    a_copy(0).wait_recv()
    sent[1, top] = (part[:tall] + got_a[0, top].astype(F32)).astype(BF16)
    a_copy(1).start()
    part = piece(2)
    sent[2, top] = part[:tall].astype(BF16)
    b_copy(0).wait_recv()
    sent[2, low] = (part[tall:] + got_b[0, low].astype(F32)).astype(BF16)
    b_copy(1).start()
    yield
    for hop in (2, 3):
        part = piece(2 * hop - 1)
        a_copy(hop - 1).wait_recv()
        sent[2 * hop - 1] = (part + got_a[hop - 1].astype(F32)).astype(BF16)
        a_copy(hop).start()
        part = piece(2 * hop)
        b_copy(hop - 1).wait_recv()
        sent[2 * hop] = (part + got_b[hop - 1].astype(F32)).astype(BF16)
        b_copy(hop).start()
        yield
    part = piece(7)
    a_copy(3).wait_recv()
    b_copy(3).wait_recv()
    total = part + got_a[3].astype(F32) + got_b[3].astype(F32)
    yield total
    for hop in range(4):
        a_copy(hop).wait_send()
        b_copy(hop).wait_send()
    yield


def layer_kernel(
    scale,
    row_prev, row_last, col_prev, col_last, rows, cols,
    feats_h, vals_h, dst_h, cot_h, w_self_h, w_neigh_h,
    out, w_out, source,
    feats, vals, dst, cot, w_self, w_neigh, sums, grads,
    c_send, got_c, x_send, got_x, z_sent, z_a, z_b,
    h_send, got_h, y_sent, y_a, y_b,
    w_full, w_c, w_xs, w_x, w_zs, w_z, w_mine, w_rows,
    load_sem,
    c_s, c_r, x_s, x_r, za_s, za_r, zb_s, zb_r, h_s, h_r, ya_s, ya_r, yb_s, yb_r,
    ga_s, ga_r, gb_s, gb_r, gx_s, gx_r, gc_s, gc_r,
    wc_s, wc_r, wx_s, wx_r, wz_s, wz_r, wr_s, wr_r, wg_s, wg_r, wl_s, wl_r,
):
    row, col = lax.axis_index("row"), lax.axis_index("col")
    z, x, k = col // 4, (col // 2) % 2, col % 2
    y, h = row // 2, row % 2
    slots = vals.shape[0]
    quarter = slots // 4

    def at_col(zz, xx, kk):
        return (row, (zz % N) * 4 + xx * 2 + kk)

    def at_row(yy, hh):
        return ((yy % N) * 2 + hh, col)

    sibling, beside, across = at_col(z, x, 1 - k), at_col(z, 1 - x, k), at_row(y, 1 - h)

    def near(i):
        return at_col(z + i % N, (x + i // N) % 2, k)

    def far(i):
        return at_row(y + i % N, (h + i // N) % 2)

    barrier = pltpu.get_barrier_semaphore()

    def greet(i, c):
        pl.semaphore_signal(barrier, inc=1, device_id=near(i), device_id_type=MESH)
        pl.semaphore_signal(barrier, inc=1, device_id=far(i), device_id_type=MESH)
        return c

    pl.semaphore_signal(barrier, inc=1, device_id=sibling, device_id_type=MESH)
    lax.fori_loop(1, 2 * N, greet, 0)

    loads = [pltpu.make_async_copy(feats_h, feats, load_sem.at[0])]
    for i in range(4):
        part = pl.ds(i * quarter, quarter)
        loads.append(pltpu.make_async_copy(vals_h.at[part], vals.at[part], load_sem.at[1 + i]))
    for i, (src, dest) in enumerate(((dst_h, dst), (w_self_h, w_self), (w_neigh_h, w_neigh), (cot_h, cot))):
        loads.append(pltpu.make_async_copy(src, dest, load_sem.at[5 + i]))
    for load in loads:
        load.start()

    sums[slots] = jnp.zeros_like(sums[slots])
    loads[0].wait()
    for s in range(slots):
        if s % quarter == 0:
            loads[1 + s // quarter].wait()
        sums[s] = sums[row_prev[s]] + jnp.dot(vals[s], feats[cols[0, 0, s]], preferred_element_type=F32)

    def partial(zz, xx, kk):
        return sums[row_last[(zz % N) * 4 + xx * 2 + kk]]

    pl.semaphore_wait(barrier, 4 * N - 1)

    def c_copy(i):
        return remote(c_send.at[i], got_c.at[i], c_s.at[i], c_r.at[i], sibling)

    for i in range(2 * N):
        c_send[i] = partial(z + OFFSETS[i % N], 1 - x if i < N else x, 1 - k).astype(BF16)
        c_copy(i).start()

    def x_copy(i):
        return remote(x_send.at[i], got_x.at[i], x_s.at[i], x_r.at[i], beside)

    for i in range(N):
        own = partial(z + OFFSETS[i], 1 - x, k)
        c_copy(i).wait_recv()
        x_send[i] = (own + got_c[i].astype(F32)).astype(BF16)
        x_copy(i).start()

    for load in loads[5:]:
        load.wait()
    pre_self = jnp.dot(dst[...], w_self[...], preferred_element_type=F32)

    def col_piece(i):
        own = partial(z + OFFSETS[i], x, k)
        c_copy(N + i).wait_recv()
        own += got_c[N + i].astype(F32)
        x_copy(i).wait_recv()
        return own + got_x[i].astype(F32)

    z_next, z_back = at_col(z + 1, x, k), at_col(z + N - 1, x, k)
    z_ring = ring_reduce(col_piece, z_next, z_back, z_sent, z_a, z_b, za_s, za_r, zb_s, zb_r)
    for _ in range(3):
        next(z_ring)
    agg = next(z_ring).astype(BF16)

    pre = pre_self + jnp.dot(agg, w_neigh[...], preferred_element_type=F32)
    sig = jax.nn.sigmoid(pre)
    gpre = (cot[...].astype(F32) * sig * (1.0 + pre * (1.0 - sig))).astype(BF16)
    mine = k * 2 * N + x * N
    me = mine + z
    grads[me] = lax.dot_general(
        gpre, w_neigh[...], (((1,), (1,)), ((), ())), preferred_element_type=F32
    ).astype(BF16)

    tall = grads.shape[1] // 2
    top, low = pl.ds(0, tall), pl.ds(tall, tall)

    def ga_copy(hop):
        slot = mine + (z + N - hop) % N
        ref = grads.at[slot, top] if hop == 3 else grads.at[slot]
        return remote(ref, ref, ga_s.at[hop], ga_r.at[hop], z_next)

    def gb_copy(hop):
        slot = mine + (z + hop) % N
        ref = grads.at[slot, low] if hop == 3 else grads.at[slot]
        return remote(ref, ref, gb_s.at[hop], gb_r.at[hop], z_back)

    def gx_copy(off):
        ref = grads.at[mine + (z + off) % N]
        return remote(ref, ref, gx_s.at[off], gx_r.at[off], beside)

    def gc_copy(other, off):
        ref = grads.at[k * 2 * N + ((x + other) % 2) * N + (z + off) % N]
        return remote(ref, ref, gc_s.at[other * N + off], gc_r.at[other * N + off], sibling)

    def spread(off):
        gx_copy(off).start()
        gc_copy(0, off).start()

    def from_beside(off):
        gx_copy(off).wait_recv()
        gc_copy(1, off).start()

    ga_copy(0).start()
    gb_copy(0).start()
    spread(0)
    out[...] = (pre * sig).astype(BF16)

    feat = dst.shape[1]
    pieces, wide, hid = w_full.shape
    half = pieces // 2
    for base, left in ((0, dst[...]), (1, agg)):
        dw = lax.dot_general(left, gpre, (((0,), (0,)), ((), ())), preferred_element_type=F32)
        w_full[pl.ds(base * half, half)] = dw.reshape(half, wide, hid)
    wc_copy = remote(w_full.at[pl.ds((1 - k) * half, half)], w_c, wc_s, wc_r, sibling)
    wc_copy.start()

    for hop in (1, 2, 3):
        ga_copy(hop - 1).wait_recv()
        ga_copy(hop).start()
        spread(N - hop)
        gb_copy(hop - 1).wait_recv()
        gb_copy(hop).start()
        spread(hop)
        if hop == 1:
            from_beside(0)
            wc_copy.wait_recv()
            w_xs[...] = w_full[pl.ds(k * half + (1 - x) * N, N)] + w_c[pl.ds((1 - x) * N, N)]
            wx_copy = remote(w_xs, w_x, wx_s, wx_r, beside)
            wx_copy.start()
        else:
            from_beside(N - hop + 1)
            from_beside(hop - 1)
    wx_copy.wait_recv()
    w_zs[...] = w_full[pl.ds(k * half + x * N, N)] + w_c[pl.ds(x * N, N)] + w_x[...]

    def wz_copy(d):
        ref = w_zs.at[(z + d) % N]
        return remote(ref, w_z.at[z], wz_s.at[d], wz_r.at[d], near(d))

    for d in OFFSETS[:-1]:
        wz_copy(d).start()
    ga_copy(3).wait_recv()
    gb_copy(3).wait_recv()
    spread(4)
    for off in (5, 3, 4):
        from_beside(off)
    for i in range(2 * N):
        gc_copy(i // N, i % N).wait_recv()

    for s in range(slots):
        r = rows[0, 0, s]
        g = grads[(r % 2) * 2 * N + ((r // 2) % 2) * N + r // 4]
        sums[s] = sums[col_prev[s]] + lax.dot_general(
            vals[s], g, (((0,), (0,)), ((), ())), preferred_element_type=F32
        )

    def source_partial(yy, hh):
        return sums[col_last[(yy % N) * 2 + hh]]

    def h_copy(i):
        return remote(h_send.at[i], got_h.at[i], h_s.at[i], h_r.at[i], across)

    for i in range(N):
        h_send[i] = source_partial(y + OFFSETS[i], 1 - h).astype(BF16)
        h_copy(i).start()

    total = w_zs[z]
    for d in range(1, N):
        wz_copy(d).wait_recv()
        total += w_z[(z + N - d) % N]
    w_mine[...] = total
    w_rows[row] = total

    def wr_copy(i):
        return remote(w_mine, w_rows.at[row], wr_s.at[i], wr_r.at[i], far(i))

    for i in range(1, 2 * N):
        wr_copy(i).start()

    def row_piece(i):
        own = source_partial(y + OFFSETS[i], h)
        h_copy(i).wait_recv()
        return own + got_h[i].astype(F32)

    y_ring = ring_reduce(
        row_piece, at_row(y + 1, h), at_row(y + N - 1, h), y_sent, y_a, y_b, ya_s, ya_r, yb_s, yb_r
    )
    for _ in range(3):
        next(y_ring)
    for i in range(1, 2 * N):
        wr_copy(i).wait_recv()
    total = w_rows[0]
    for i in range(1, 2 * N):
        total += w_rows[i]
    w_out[me] = total * scale

    def wg_copy(i):
        return remote(w_out.at[me], w_out.at[me], wg_s.at[i], wg_r.at[i], near(i))

    for i in range(1, 2 * N):
        wg_copy(i).start()
    source[...] = next(y_ring)
    for i in range(1, 2 * N):
        wg_copy(i).wait_recv()
    ref = w_out.at[pl.ds(k * half, half)]
    wl_copy = remote(ref, ref, wl_s, wl_r, sibling)
    wl_copy.start()

    next(z_ring)
    next(y_ring)
    for i in range(N):
        x_copy(i).wait_send()
        h_copy(i).wait_send()
        gx_copy(i).wait_send()
    for hop in range(4):
        ga_copy(hop).wait_send()
        gb_copy(hop).wait_send()
    for i in range(2 * N):
        c_copy(i).wait_send()
        gc_copy(i // N, i % N).wait_send()
    wc_copy.wait_send()
    wx_copy.wait_send()
    for d in range(1, N):
        wz_copy(d).wait_send()
    for i in range(1, 2 * N):
        wr_copy(i).wait_send()
        wg_copy(i).wait_send()
    wl_copy.wait()


def layer(scale, tables, rows, cols, feats, vals, dst, cot, w_self, w_neigh):
    slots, block, _ = vals.shape
    width = feats.shape[-1]
    hid = w_self.shape[1]
    wide = 2 * width // (4 * N)

    def blocks(n, kind=BF16):
        return pltpu.VMEM((n, block, width), kind)

    def slabs(n):
        return pltpu.VMEM((n, wide, hid), F32)

    return pl.pallas_call(
        functools.partial(layer_kernel, scale),
        out_shape=(
            jax.ShapeDtypeStruct((block, hid), BF16),
            jax.ShapeDtypeStruct((4 * N, wide, hid), F32),
            jax.ShapeDtypeStruct((block, width), F32),
        ),
        in_specs=[SMEM] * 6 + [HBM] * 6,
        out_specs=(VMEM,) * 3,
        scratch_shapes=[
            blocks(feats.shape[0]), pltpu.VMEM(vals.shape, BF16), pltpu.VMEM(dst.shape, BF16),
            pltpu.VMEM(cot.shape, BF16), pltpu.VMEM(w_self.shape, BF16), pltpu.VMEM(w_neigh.shape, BF16),
            blocks(slots + 1, F32), blocks(4 * N),
            blocks(2 * N), blocks(2 * N), blocks(N), blocks(N), blocks(N - 1), blocks(4), blocks(4),
            blocks(N), blocks(N), blocks(N - 1), blocks(4), blocks(4),
            slabs(4 * N), slabs(2 * N), slabs(N), slabs(N), slabs(N), slabs(N),
            pltpu.VMEM((wide, hid), F32), slabs(2 * N),
            DMA((9,)),
            DMA((2 * N,)), DMA((2 * N,)), DMA((N,)), DMA((N,)), DMA((4,)), DMA((4,)), DMA((4,)), DMA((4,)),
            DMA((N,)), DMA((N,)), DMA((4,)), DMA((4,)), DMA((4,)), DMA((4,)),
            DMA((4,)), DMA((4,)), DMA((4,)), DMA((4,)), DMA((N,)), DMA((N,)), DMA((2 * N,)), DMA((2 * N,)),
            DMA, DMA, DMA, DMA, DMA((N,)), DMA((N,)), DMA((2 * N,)), DMA((2 * N,)), DMA((2 * N,)), DMA((2 * N,)),
            DMA, DMA,
        ],
        compiler_params=pltpu.CompilerParams(
            collective_id=0, has_side_effects=True, vmem_limit_bytes=40 * 1024 * 1024
        ),
    )(*tables, rows, cols, feats, vals, dst, cot, w_self, w_neigh)


def per_device(features, dst_features, w_self, w_neigh, cotangent, block_values, block_rows, block_cols, block_counts):
    block = block_values.shape[-1]
    width = features.shape[-1]
    tables = chains(block_rows, block_cols, block_counts, 4 * N, 2 * N)
    nodes = dst_features.shape[0] * lax.axis_size("row") * lax.axis_size("col")
    out, w_all, source = layer(
        1.0 / math.sqrt(nodes), tables, block_rows, block_cols, features.reshape(-1, block, width),
        block_values[0, 0], dst_features, cotangent, w_self, w_neigh,
    )
    w_all = w_all.reshape(2, width, -1)
    return out, w_all[0], w_all[1], source[None]


def solution(mesh):
    placed = (
        P("col", None, None),
        P(("row", "col"), None),
        P(),
        P(),
        P(("row", "col"), None),
        P("row", "col", None, None, None),
        P("row", "col", None),
        P("row", "col", None),
        P("row", "col"),
    )
    return jax.shard_map(
        per_device,
        mesh=mesh,
        in_specs=placed,
        out_specs=(P(("row", "col"), None), P(), P(), P("col", "row", None)),
        check_vma=False,
    )
```

```python
import functools
import math

import jax
import jax.numpy as jnp
from jax import lax
from jax.experimental import pallas as pl
from jax.experimental.pallas import tpu as pltpu
from jax.sharding import PartitionSpec as P

BF16 = jnp.bfloat16
F32 = jnp.float32
MESH = pl.DeviceIdType.MESH
N = 8
OFFSETS = (4, 3, 5, 2, 6, 1, 7, 0)
SPREAD = (1, 7, 2, 6, 3, 5, 4)
VMEM = pl.BlockSpec(memory_space=pltpu.VMEM)
SMEM = pl.BlockSpec(memory_space=pltpu.SMEM)
HBM = pl.BlockSpec(memory_space=pltpu.HBM)
DMA = pltpu.SemaphoreType.DMA


class Copies:
    def __init__(self):
        self.started = []

    def __call__(self, src, dst, send, recv, device):
        return pltpu.make_async_remote_copy(
            src_ref=src, dst_ref=dst, send_sem=send, recv_sem=recv, device_id=device, device_id_type=MESH
        )

    def start(self, copy):
        copy.start()
        self.started.append(copy)

    def finish(self):
        for copy in self.started:
            copy.wait_send()


def chain_kernel(rows, cols, counts, row_prev, row_last, col_prev, col_last):
    slots = row_prev.shape[0]
    live = counts[0, 0]
    for last in (row_last, col_last):
        for b in range(last.shape[0]):
            last[b] = slots
    for s in range(slots):
        for ids, prev, last in ((rows, row_prev, row_last), (cols, col_prev, col_last)):
            b = ids[0, 0, s]
            before = last[b]
            prev[s] = before
            last[b] = jnp.where(s < live, s, before)


def chains(rows, cols, counts, row_blocks, col_blocks):
    slots = rows.shape[-1]
    return pl.pallas_call(
        chain_kernel,
        out_shape=tuple(jax.ShapeDtypeStruct((n,), jnp.int32) for n in (slots, row_blocks, slots, col_blocks)),
        in_specs=[SMEM] * 3,
        out_specs=(SMEM,) * 4,
    )(rows, cols, counts)


def layer_kernel(
    scale,
    row_prev, row_last, col_prev, col_last, rows, cols,
    feats_h, vals_h, dst_h, cot_h, w_self_h, w_neigh_h,
    out, w_out, source,
    feats, vals, dst, cot, w_self, w_neigh, sums, grads,
    c_send, got_c, x_send, got_x, z_send, got_z,
    h_send, got_h, y_send, got_y,
    w_full, w_c, w_xs, w_x, w_zs, w_z, w_mine, w_rows,
    load_sem,
    c_s, c_r, x_s, x_r, z_s, z_r, h_s, h_r, y_s, y_r,
    gz_s, gz_r, gx_s, gx_r, gc_s, gc_r,
    wc_s, wc_r, wx_s, wx_r, wz_s, wz_r, wr_s, wr_r, wg_s, wg_r, wl_s, wl_r,
):
    remote = Copies()
    row, col = lax.axis_index("row"), lax.axis_index("col")
    z, x, k = col // 4, (col // 2) % 2, col % 2
    y, h = row // 2, row % 2
    slots = vals.shape[0]
    quarter = slots // 4

    def at_col(zz, xx, kk):
        return (row, (zz % N) * 4 + xx * 2 + kk)

    def at_row(yy, hh):
        return ((yy % N) * 2 + hh, col)

    sibling, beside, across = at_col(z, x, 1 - k), at_col(z, 1 - x, k), at_row(y, 1 - h)

    def near(i):
        return at_col(z + i % N, (x + i // N) % 2, k)

    def far(i):
        return at_row(y + i % N, (h + i // N) % 2)

    barrier = pltpu.get_barrier_semaphore()

    def wz_copy(d):
        ref = w_zs.at[(z + d) % N]
        return remote(ref, w_z.at[z], wz_s.at[d], wz_r.at[d], near(d))

    def greet(i, c):
        pl.semaphore_signal(barrier, inc=1, device_id=near(i), device_id_type=MESH)
        pl.semaphore_signal(barrier, inc=1, device_id=far(i), device_id_type=MESH)
        return c

    pl.semaphore_signal(barrier, inc=1, device_id=sibling, device_id_type=MESH)
    lax.fori_loop(1, 2 * N, greet, 0)

    loads = [pltpu.make_async_copy(feats_h, feats, load_sem.at[0])]
    for i in range(4):
        part = pl.ds(i * quarter, quarter)
        loads.append(pltpu.make_async_copy(vals_h.at[part], vals.at[part], load_sem.at[1 + i]))
    for i, (src, dest) in enumerate(((dst_h, dst), (w_self_h, w_self), (w_neigh_h, w_neigh), (cot_h, cot))):
        loads.append(pltpu.make_async_copy(src, dest, load_sem.at[5 + i]))
    for load in loads:
        load.start()

    sums[slots] = jnp.zeros_like(sums[slots])
    loads[0].wait()
    for s in range(slots):
        if s % quarter == 0:
            loads[1 + s // quarter].wait()
        sums[s] = sums[row_prev[s]] + jnp.dot(vals[s], feats[cols[0, 0, s]], preferred_element_type=F32)

    def partial(zz, xx, kk):
        return sums[row_last[(zz % N) * 4 + xx * 2 + kk]]

    pl.semaphore_wait(barrier, 4 * N - 1)

    def c_copy(i):
        return remote(c_send.at[i], got_c.at[i], c_s.at[i], c_r.at[i], sibling)

    for i in range(2 * N):
        c_send[i] = partial(z + OFFSETS[i % N], 1 - x if i < N else x, 1 - k).astype(BF16)
        remote.start(c_copy(i))

    def x_copy(i):
        return remote(x_send.at[i], got_x.at[i], x_s.at[i], x_r.at[i], beside)

    for i in range(N):
        own = partial(z + OFFSETS[i], 1 - x, k)
        c_copy(i).wait_recv()
        x_send[i] = (own + got_c[i].astype(F32)).astype(BF16)
        remote.start(x_copy(i))

    for load in loads[5:]:
        load.wait()
    pre_self = jnp.dot(dst[...], w_self[...], preferred_element_type=F32)

    def col_piece(i):
        own = partial(z + OFFSETS[i], x, k)
        c_copy(N + i).wait_recv()
        own += got_c[N + i].astype(F32)
        x_copy(i).wait_recv()
        return own + got_x[i].astype(F32)

    def z_copy(i):
        return remote(z_send.at[i], got_z.at[i], z_s.at[i], z_r.at[i], at_col(z + OFFSETS[i], x, k))

    for i in range(N - 1):
        z_send[i] = col_piece(i).astype(BF16)
        remote.start(z_copy(i))
    total = col_piece(N - 1)
    for i in range(N - 1):
        z_copy(i).wait_recv()
        total += got_z[i].astype(F32)
    agg = total.astype(BF16)

    pre = pre_self + jnp.dot(agg, w_neigh[...], preferred_element_type=F32)
    sig = jax.nn.sigmoid(pre)
    gpre = (cot[...].astype(F32) * sig * (1.0 + pre * (1.0 - sig))).astype(BF16)
    mine = k * 2 * N + x * N
    me = mine + z
    grads[me] = lax.dot_general(
        gpre, w_neigh[...], (((1,), (1,)), ((), ())), preferred_element_type=F32
    ).astype(BF16)

    def gz_copy(i):
        ref = grads.at[me]
        return remote(ref, ref, gz_s.at[i], gz_r.at[i], at_col(z + SPREAD[i], x, k))

    def gx_copy(off):
        ref = grads.at[mine + (z + N - off) % N]
        return remote(ref, ref, gx_s.at[off], gx_r.at[off], beside)

    def gc_copy(other, off):
        ref = grads.at[k * 2 * N + ((x + other) % 2) * N + (z + N - off) % N]
        return remote(ref, ref, gc_s.at[other * N + off], gc_r.at[other * N + off], sibling)

    for i in range(N - 1):
        remote.start(gz_copy(i))
    remote.start(gx_copy(0))
    remote.start(gc_copy(0, 0))
    out[...] = (pre * sig).astype(BF16)

    feat = dst.shape[1]
    pieces, wide, hid = w_full.shape
    half = pieces // 2
    for base, left in ((0, dst[...]), (1, agg)):
        dw = lax.dot_general(left, gpre, (((0,), (0,)), ((), ())), preferred_element_type=F32)
        w_full[pl.ds(base * half, half)] = dw.reshape(half, wide, hid)
    wc_copy = remote(w_full.at[pl.ds((1 - k) * half, half)], w_c, wc_s, wc_r, sibling)
    wx_copy = remote(w_xs, w_x, wx_s, wx_r, beside)
    remote.start(wc_copy)

    def from_beside(off):
        gx_copy(off).wait_recv()
        remote.start(gc_copy(1, off))

    for i, off in enumerate(SPREAD):
        gz_copy(i).wait_recv()
        remote.start(gx_copy(off))
        remote.start(gc_copy(0, off))
        if i == 1:
            wc_copy.wait_recv()
            w_xs[...] = w_full[pl.ds(k * half + (1 - x) * N, N)] + w_c[pl.ds((1 - x) * N, N)]
            remote.start(wx_copy)
        if i == 3:
            from_beside(0)
    for i, off in enumerate(SPREAD):
        from_beside(off)
        if i == 3:
            wx_copy.wait_recv()
            w_zs[...] = w_full[pl.ds(k * half + x * N, N)] + w_c[pl.ds(x * N, N)] + w_x[...]
            for d in range(1, N):
                remote.start(wz_copy(d))
    for i in range(2 * N):
        gc_copy(i // N, i % N).wait_recv()

    for s in range(slots):
        r = rows[0, 0, s]
        g = grads[(r % 2) * 2 * N + ((r // 2) % 2) * N + r // 4]
        sums[s] = sums[col_prev[s]] + lax.dot_general(
            vals[s], g, (((0,), (0,)), ((), ())), preferred_element_type=F32
        )

    def source_partial(yy, hh):
        return sums[col_last[(yy % N) * 2 + hh]]

    def h_copy(i):
        return remote(h_send.at[i], got_h.at[i], h_s.at[i], h_r.at[i], across)

    for i in range(N):
        h_send[i] = source_partial(y + OFFSETS[i], 1 - h).astype(BF16)
        remote.start(h_copy(i))

    total = w_zs[z]
    for d in range(1, N):
        wz_copy(d).wait_recv()
        total += w_z[(z + N - d) % N]
    w_mine[...] = total
    w_rows[row] = total

    def wr_copy(i):
        return remote(w_mine, w_rows.at[row], wr_s.at[i], wr_r.at[i], far(i))

    for i in range(1, 2 * N):
        remote.start(wr_copy(i))

    def y_copy(i):
        return remote(y_send.at[i], got_y.at[i], y_s.at[i], y_r.at[i], at_row(y + OFFSETS[i], h))

    def row_piece(i):
        own = source_partial(y + OFFSETS[i], h)
        h_copy(i).wait_recv()
        return own + got_h[i].astype(F32)

    for i in range(N - 1):
        y_send[i] = row_piece(i).astype(BF16)
        remote.start(y_copy(i))

    for i in range(1, 2 * N):
        wr_copy(i).wait_recv()
    total = w_rows[0]
    for i in range(1, 2 * N):
        total += w_rows[i]
    w_out[me] = total * scale

    def wg_copy(i):
        return remote(w_out.at[me], w_out.at[me], wg_s.at[i], wg_r.at[i], near(i))

    for i in range(1, 2 * N):
        remote.start(wg_copy(i))

    total = row_piece(N - 1)
    for i in range(N - 1):
        y_copy(i).wait_recv()
        total += got_y[i].astype(F32)
    source[...] = total

    for i in range(1, 2 * N):
        wg_copy(i).wait_recv()
    ref = w_out.at[pl.ds(k * half, half)]
    wl_copy = remote(ref, ref, wl_s, wl_r, sibling)
    remote.start(wl_copy)
    wl_copy.wait_recv()
    remote.finish()


def layer(scale, tables, rows, cols, feats, vals, dst, cot, w_self, w_neigh):
    slots, block, _ = vals.shape
    width = feats.shape[-1]
    hid = w_self.shape[1]
    wide = 2 * width // (4 * N)

    def blocks(n, kind=BF16):
        return pltpu.VMEM((n, block, width), kind)

    def slabs(n):
        return pltpu.VMEM((n, wide, hid), F32)

    return pl.pallas_call(
        functools.partial(layer_kernel, scale),
        out_shape=(
            jax.ShapeDtypeStruct((block, hid), BF16),
            jax.ShapeDtypeStruct((4 * N, wide, hid), F32),
            jax.ShapeDtypeStruct((block, width), F32),
        ),
        in_specs=[SMEM] * 6 + [HBM] * 6,
        out_specs=(VMEM,) * 3,
        scratch_shapes=[
            blocks(feats.shape[0]), pltpu.VMEM(vals.shape, BF16), pltpu.VMEM(dst.shape, BF16),
            pltpu.VMEM(cot.shape, BF16), pltpu.VMEM(w_self.shape, BF16), pltpu.VMEM(w_neigh.shape, BF16),
            blocks(slots + 1, F32), blocks(4 * N),
            blocks(2 * N), blocks(2 * N), blocks(N), blocks(N), blocks(N - 1), blocks(N - 1),
            blocks(N), blocks(N), blocks(N - 1), blocks(N - 1),
            slabs(4 * N), slabs(2 * N), slabs(N), slabs(N), slabs(N), slabs(N),
            pltpu.VMEM((wide, hid), F32), slabs(2 * N),
            DMA((9,)),
            DMA((2 * N,)), DMA((2 * N,)), DMA((N,)), DMA((N,)), DMA((N,)), DMA((N,)),
            DMA((N,)), DMA((N,)), DMA((N,)), DMA((N,)),
            DMA((N,)), DMA((N,)), DMA((N,)), DMA((N,)), DMA((2 * N,)), DMA((2 * N,)),
            DMA, DMA, DMA, DMA, DMA((N,)), DMA((N,)), DMA((2 * N,)), DMA((2 * N,)), DMA((2 * N,)), DMA((2 * N,)),
            DMA, DMA,
        ],
        compiler_params=pltpu.CompilerParams(
            collective_id=0, has_side_effects=True, vmem_limit_bytes=60 * 1024 * 1024
        ),
    )(*tables, rows, cols, feats, vals, dst, cot, w_self, w_neigh)


def per_device(features, dst_features, w_self, w_neigh, cotangent, block_values, block_rows, block_cols, block_counts):
    block = block_values.shape[-1]
    width = features.shape[-1]
    tables = chains(block_rows, block_cols, block_counts, 4 * N, 2 * N)
    nodes = dst_features.shape[0] * lax.axis_size("row") * lax.axis_size("col")
    out, w_all, source = layer(
        1.0 / math.sqrt(nodes), tables, block_rows, block_cols, features.reshape(-1, block, width),
        block_values[0, 0], dst_features, cotangent, w_self, w_neigh,
    )
    w_all = w_all.reshape(2, width, -1)
    return out, w_all[0], w_all[1], source[None]


def solution(mesh):
    placed = (
        P("col", None, None),
        P(("row", "col"), None),
        P(),
        P(),
        P(("row", "col"), None),
        P("row", "col", None, None, None),
        P("row", "col", None),
        P("row", "col", None),
        P("row", "col"),
    )
    return jax.shard_map(
        per_device,
        mesh=mesh,
        in_specs=placed,
        out_specs=(P(("row", "col"), None), P(), P(), P("col", "row", None)),
        check_vma=False,
    )
```

```python
import functools
import math

import jax
import jax.numpy as jnp
from jax import lax
from jax.experimental import pallas as pl
from jax.experimental.pallas import tpu as pltpu
from jax.sharding import PartitionSpec as P

BF16 = jnp.bfloat16
F32 = jnp.float32
MESH = pl.DeviceIdType.MESH
N = 8
OFFSETS = (4, 3, 5, 2, 6, 1, 7, 0)
SPREAD = (1, 7, 2, 6, 3, 5, 4)
SMEM = pl.BlockSpec(memory_space=pltpu.SMEM)
HBM = pl.BlockSpec(memory_space=pltpu.HBM)
DMA = pltpu.SemaphoreType.DMA


class Copies:
    def __init__(self):
        self.started = []

    def __call__(self, src, dst, send, recv, device):
        return pltpu.make_async_remote_copy(
            src_ref=src, dst_ref=dst, send_sem=send, recv_sem=recv, device_id=device, device_id_type=MESH
        )

    def start(self, copy):
        copy.start()
        self.started.append(copy)

    def finish(self):
        for copy in self.started:
            copy.wait_send()


def chain(ids, live):
    slots = ids.shape[1]
    t = lax.broadcasted_iota(jnp.int32, (slots, slots), 0)
    s = lax.broadcasted_iota(jnp.int32, (slots, slots), 1)
    along = jnp.broadcast_to(ids, (slots, slots))
    down = jnp.sum(jnp.where(t == s, along, 0), axis=1, keepdims=True)
    used = t < live
    prev = jnp.max(jnp.where((down == along) & (t < s) & used, t, -1), axis=0, keepdims=True)
    last = jnp.max(jnp.where((down == s) & used, t, -1), axis=0, keepdims=True)
    return jnp.where(prev < 0, slots, prev), jnp.where(last < 0, slots, last)


def layer_kernel(
    scale,
    rows_h, cols_h, counts, feats_h, vals_h, dst_h, cot_h, w_self_h, w_neigh_h,
    out_h, w_out_h, source_h,
    rows, cols, tables, table, out, w_out, source, feats, vals, dst, cot, w_self, w_neigh, sums, grads,
    c_send, got_c, x_send, got_x, z_send, got_z,
    h_send, got_h, y_send, got_y,
    w_full, w_c, w_xs, w_x, w_zs, w_z, w_mine, w_rows,
    load_sem, table_sem, store_sem,
    c_s, c_r, x_s, x_r, z_s, z_r, h_s, h_r, y_s, y_r,
    gz_s, gz_r, gx_s, gx_r, gc_s, gc_r,
    wc_s, wc_r, wx_s, wx_r, wz_s, wz_r, wr_s, wr_r, wg_s, wg_r, wl_s, wl_r,
):
    remote = Copies()
    row, col = lax.axis_index("row"), lax.axis_index("col")
    z, x, k = col // 4, (col // 2) % 2, col % 2
    y, h = row // 2, row % 2
    slots = vals.shape[0]
    quarter = slots // 4

    def at_col(zz, xx, kk):
        return (row, (zz % N) * 4 + xx * 2 + kk)

    def at_row(yy, hh):
        return ((yy % N) * 2 + hh, col)

    mine = k * 2 * N + x * N
    me = mine + z
    sibling, beside, across = at_col(z, x, 1 - k), at_col(z, 1 - x, k), at_row(y, 1 - h)

    def near(i):
        return at_col(z + i % N, (x + i // N) % 2, k)

    def far(i):
        return at_row(y + i % N, (h + i // N) % 2)

    barrier = pltpu.get_barrier_semaphore()

    def wz_copy(d):
        ref = w_zs.at[(z + d) % N]
        return remote(ref, w_z.at[z], wz_s.at[d], wz_r.at[d], near(d))

    def wr_copy(i):
        return remote(w_mine, w_rows.at[row], wr_s.at[i], wr_r.at[i], far(i))

    def wg_copy(i):
        return remote(w_out.at[me], w_out.at[me], wg_s.at[i], wg_r.at[i], near(i))

    def greet(i, c):
        pl.semaphore_signal(barrier, inc=1, device_id=near(i), device_id_type=MESH)
        pl.semaphore_signal(barrier, inc=1, device_id=far(i), device_id_type=MESH)
        return c

    pl.semaphore_signal(barrier, inc=1, device_id=sibling, device_id_type=MESH)
    lax.fori_loop(1, 2 * N, greet, 0)

    loads = []
    for i, (src, dest) in enumerate(((rows_h, rows), (cols_h, cols), (feats_h, feats))):
        loads.append(pltpu.make_async_copy(src, dest, load_sem.at[i]))
    for i in range(4):
        part = pl.ds(i * quarter, quarter)
        loads.append(pltpu.make_async_copy(vals_h.at[part], vals.at[part], load_sem.at[3 + i]))
    for i, (src, dest) in enumerate(((dst_h, dst), (w_self_h, w_self), (w_neigh_h, w_neigh), (cot_h, cot))):
        loads.append(pltpu.make_async_copy(src, dest, load_sem.at[7 + i]))
    for load in loads:
        load.start()

    sums[slots] = jnp.zeros_like(sums[slots])
    tables[...] = jnp.zeros_like(tables)
    for load in loads[:2]:
        load.wait()
    r, c = rows[...], cols[...]
    row_prev, row_last = chain(r, counts[0, 0])
    col_prev, col_last = chain(c, counts[0, 0])
    at = (r % 2) * (2 * N) + ((r // 2) % 2) * N + r // 4
    for i, line in enumerate((row_prev, row_last, col_prev, col_last, c, at)):
        tables[pl.ds(i, 1), pl.ds(0, slots)] = line
    to_scalars = pltpu.make_async_copy(tables, table, table_sem)
    to_scalars.start()
    to_scalars.wait()

    loads[2].wait()
    for s in range(slots):
        if s % quarter == 0:
            loads[3 + s // quarter].wait()
        sums[s] = sums[table[0, s]] + jnp.dot(vals[s], feats[table[4, s]], preferred_element_type=F32)

    def partial(zz, xx, kk):
        return sums[table[1, (zz % N) * 4 + xx * 2 + kk]]

    pl.semaphore_wait(barrier, 4 * N - 1)

    def c_copy(i):
        return remote(c_send.at[i], got_c.at[i], c_s.at[i], c_r.at[i], sibling)

    for i in range(2 * N):
        c_send[i] = partial(z + OFFSETS[i % N], 1 - x if i < N else x, 1 - k).astype(BF16)
        remote.start(c_copy(i))

    def x_copy(i):
        return remote(x_send.at[i], got_x.at[i], x_s.at[i], x_r.at[i], beside)

    for i in range(N):
        own = partial(z + OFFSETS[i], 1 - x, k)
        c_copy(i).wait_recv()
        x_send[i] = (own + got_c[i].astype(F32)).astype(BF16)
        remote.start(x_copy(i))

    for load in loads[7:]:
        load.wait()
    pre_self = jnp.dot(dst[...], w_self[...], preferred_element_type=F32)

    def col_piece(i):
        own = partial(z + OFFSETS[i], x, k)
        c_copy(N + i).wait_recv()
        own += got_c[N + i].astype(F32)
        x_copy(i).wait_recv()
        return own + got_x[i].astype(F32)

    def z_copy(i):
        return remote(z_send.at[i], got_z.at[i], z_s.at[i], z_r.at[i], at_col(z + OFFSETS[i], x, k))

    for i in range(N - 1):
        z_send[i] = col_piece(i).astype(BF16)
        remote.start(z_copy(i))
    total = col_piece(N - 1)
    for i in range(N - 1):
        z_copy(i).wait_recv()
        total += got_z[i].astype(F32)
    agg = total.astype(BF16)

    pre = pre_self + jnp.dot(agg, w_neigh[...], preferred_element_type=F32)
    sig = jax.nn.sigmoid(pre)
    gpre = (cot[...].astype(F32) * sig * (1.0 + pre * (1.0 - sig))).astype(BF16)
    grads[me] = lax.dot_general(
        gpre, w_neigh[...], (((1,), (1,)), ((), ())), preferred_element_type=F32
    ).astype(BF16)

    def gz_copy(i):
        ref = grads.at[me]
        return remote(ref, ref, gz_s.at[i], gz_r.at[i], at_col(z + SPREAD[i], x, k))

    def gx_copy(off):
        ref = grads.at[mine + (z + N - off) % N]
        return remote(ref, ref, gx_s.at[off], gx_r.at[off], beside)

    def gc_copy(other, off):
        ref = grads.at[k * 2 * N + ((x + other) % 2) * N + (z + N - off) % N]
        return remote(ref, ref, gc_s.at[other * N + off], gc_r.at[other * N + off], sibling)

    for i in range(N - 1):
        remote.start(gz_copy(i))
    remote.start(gx_copy(0))
    remote.start(gc_copy(0, 0))
    out[...] = (pre * sig).astype(BF16)
    stores = [pltpu.make_async_copy(out, out_h, store_sem.at[0])]
    stores[0].start()

    feat = dst.shape[1]
    pieces, wide, hid = w_full.shape
    half = pieces // 2
    for base, left in ((0, dst[...]), (1, agg)):
        dw = lax.dot_general(left, gpre, (((0,), (0,)), ((), ())), preferred_element_type=F32)
        w_full[pl.ds(base * half, half)] = dw.reshape(half, wide, hid)
    wc_copy = remote(w_full.at[pl.ds((1 - k) * half, half)], w_c, wc_s, wc_r, sibling)
    wx_copy = remote(w_xs, w_x, wx_s, wx_r, beside)
    remote.start(wc_copy)

    def from_beside(off):
        gx_copy(off).wait_recv()
        remote.start(gc_copy(1, off))

    wc_copy.wait_recv()
    w_xs[...] = w_full[pl.ds(k * half + (1 - x) * N, N)] + w_c[pl.ds((1 - x) * N, N)]
    remote.start(wx_copy)
    for i, off in enumerate(SPREAD):
        gz_copy(i).wait_recv()
        remote.start(gx_copy(off))
        remote.start(gc_copy(0, off))
        if i == 3:
            from_beside(0)
            wx_copy.wait_recv()
            w_zs[...] = w_full[pl.ds(k * half + x * N, N)] + w_c[pl.ds(x * N, N)] + w_x[...]
            for d in range(1, N):
                remote.start(wz_copy(d))
    for off in SPREAD:
        from_beside(off)

    total = w_zs[z]
    for d in range(1, N):
        wz_copy(d).wait_recv()
        total += w_z[(z + N - d) % N]
    w_mine[...] = total
    w_rows[row] = total
    for i in range(1, 2 * N):
        remote.start(wr_copy(i))
    for i in range(2 * N):
        gc_copy(i // N, i % N).wait_recv()

    for s in range(slots):
        sums[s] = sums[table[2, s]] + lax.dot_general(
            vals[s], grads[table[5, s]], (((0,), (0,)), ((), ())), preferred_element_type=F32
        )

    def source_partial(yy, hh):
        return sums[table[3, (yy % N) * 2 + hh]]

    def h_copy(i):
        return remote(h_send.at[i], got_h.at[i], h_s.at[i], h_r.at[i], across)

    for i in range(N):
        h_send[i] = source_partial(y + OFFSETS[i], 1 - h).astype(BF16)
        remote.start(h_copy(i))

    for i in range(1, 2 * N):
        wr_copy(i).wait_recv()
    total = w_rows[0]
    for i in range(1, 2 * N):
        total += w_rows[i]
    w_out[me] = total * scale
    for i in range(1, 2 * N):
        remote.start(wg_copy(i))

    def y_copy(i):
        return remote(y_send.at[i], got_y.at[i], y_s.at[i], y_r.at[i], at_row(y + OFFSETS[i], h))

    def row_piece(i):
        own = source_partial(y + OFFSETS[i], h)
        h_copy(i).wait_recv()
        return own + got_h[i].astype(F32)

    for i in range(N - 1):
        y_send[i] = row_piece(i).astype(BF16)
        remote.start(y_copy(i))

    total = row_piece(N - 1)
    for i in range(N - 1):
        y_copy(i).wait_recv()
        total += got_y[i].astype(F32)
    source[...] = total
    stores.append(pltpu.make_async_copy(source, source_h, store_sem.at[1]))
    stores[1].start()

    for i in range(1, 2 * N):
        wg_copy(i).wait_recv()
    ref = w_out.at[pl.ds(k * half, half)]
    wl_copy = remote(ref, ref, wl_s, wl_r, sibling)
    remote.start(wl_copy)
    wl_copy.wait_recv()
    stores.append(pltpu.make_async_copy(w_out, w_out_h, store_sem.at[2]))
    stores[2].start()
    remote.finish()
    for store in stores:
        store.wait()


def layer(scale, rows, cols, counts, feats, vals, dst, cot, w_self, w_neigh):
    slots, block, _ = vals.shape
    width = feats.shape[-1]
    hid = w_self.shape[1]
    wide = 2 * width // (4 * N)
    results = (
        jax.ShapeDtypeStruct((block, hid), BF16),
        jax.ShapeDtypeStruct((4 * N, wide, hid), F32),
        jax.ShapeDtypeStruct((block, width), F32),
    )

    def like(a):
        return pltpu.VMEM(a.shape, a.dtype)

    def blocks(n, kind=BF16):
        return pltpu.VMEM((n, block, width), kind)

    def slabs(n):
        return pltpu.VMEM((n, wide, hid), F32)

    return pl.pallas_call(
        functools.partial(layer_kernel, scale),
        out_shape=results,
        in_specs=[HBM, HBM, SMEM] + [HBM] * 6,
        out_specs=(HBM,) * 3,
        scratch_shapes=[
            like(rows), like(cols), pltpu.VMEM((8, 128), jnp.int32), pltpu.SMEM((8, 128), jnp.int32),
            *map(like, results), like(feats), like(vals), like(dst), like(cot), like(w_self), like(w_neigh),
            blocks(slots + 1, F32), blocks(4 * N),
            blocks(2 * N), blocks(2 * N), blocks(N), blocks(N), blocks(N - 1), blocks(N - 1),
            blocks(N), blocks(N), blocks(N - 1), blocks(N - 1),
            slabs(4 * N), slabs(2 * N), slabs(N), slabs(N), slabs(N), slabs(N),
            pltpu.VMEM((wide, hid), F32), slabs(2 * N),
            DMA((11,)), DMA, DMA((3,)),
            DMA((2 * N,)), DMA((2 * N,)), DMA((N,)), DMA((N,)), DMA((N,)), DMA((N,)),
            DMA((N,)), DMA((N,)), DMA((N,)), DMA((N,)),
            DMA((N,)), DMA((N,)), DMA((N,)), DMA((N,)), DMA((2 * N,)), DMA((2 * N,)),
            DMA, DMA, DMA, DMA, DMA((N,)), DMA((N,)), DMA((2 * N,)), DMA((2 * N,)), DMA((2 * N,)), DMA((2 * N,)),
            DMA, DMA,
        ],
        compiler_params=pltpu.CompilerParams(
            collective_id=0, has_side_effects=True, vmem_limit_bytes=60 * 1024 * 1024
        ),
    )(rows, cols, counts, feats, vals, dst, cot, w_self, w_neigh)


def hand_kernel(out_h, w_h, source_h, out, w_self, w_neigh, source, sem):
    half = w_self.shape[0]
    pairs = (
        (out_h, out), (w_h.at[pl.ds(0, half)], w_self), (w_h.at[pl.ds(half, half)], w_neigh), (source_h, source)
    )
    copies = [pltpu.make_async_copy(src, dest, sem.at[i]) for i, (src, dest) in enumerate(pairs)]
    for copy in copies:
        copy.start()
    for copy in copies:
        copy.wait()


def hand(out, w_all, source):
    pieces, wide, hid = w_all.shape
    grad = jax.ShapeDtypeStruct((pieces // 2, wide, hid), F32)
    return pl.pallas_call(
        hand_kernel,
        out_shape=(jax.ShapeDtypeStruct(out.shape, BF16), grad, grad, jax.ShapeDtypeStruct(source.shape, F32)),
        in_specs=[HBM] * 3,
        out_specs=(HBM,) * 4,
        scratch_shapes=[DMA((4,))],
        compiler_params=pltpu.CompilerParams(vmem_limit_bytes=60 * 1024 * 1024),
    )(out, w_all, source)


def per_device(features, dst_features, w_self, w_neigh, cotangent, block_values, block_rows, block_cols, block_counts):
    block = block_values.shape[-1]
    width = features.shape[-1]
    nodes = dst_features.shape[0] * lax.axis_size("row") * lax.axis_size("col")
    results = layer(
        1.0 / math.sqrt(nodes), block_rows[0], block_cols[0], block_counts, features.reshape(-1, block, width),
        block_values[0, 0], dst_features, cotangent, w_self, w_neigh,
    )
    out, grad_self, grad_neigh, source = hand(*results)
    return out, grad_self.reshape(width, -1), grad_neigh.reshape(width, -1), source[None]


def solution(mesh):
    placed = (
        P("col", None, None),
        P(("row", "col"), None),
        P(),
        P(),
        P(("row", "col"), None),
        P("row", "col", None, None, None),
        P("row", "col", None),
        P("row", "col", None),
        P("row", "col"),
    )
    return jax.shard_map(
        per_device,
        mesh=mesh,
        in_specs=placed,
        out_specs=(P(("row", "col"), None), P(), P(), P("col", "row", None)),
        check_vma=False,
    )
```

```python
import functools
import math

import jax
import jax.numpy as jnp
from jax import lax
from jax.experimental import pallas as pl
from jax.experimental.pallas import tpu as pltpu
from jax.sharding import PartitionSpec as P

BF16 = jnp.bfloat16
F32 = jnp.float32
MESH = pl.DeviceIdType.MESH
N = 8
OFFSETS = (4, 3, 5, 2, 6, 1, 7, 0)
SPREAD = (1, 7, 2, 6, 3, 5, 4)
SMEM = pl.BlockSpec(memory_space=pltpu.SMEM)
HBM = pl.BlockSpec(memory_space=pltpu.HBM)
DMA = pltpu.SemaphoreType.DMA


class Copies:
    def __init__(self):
        self.started = []

    def __call__(self, src, dst, send, recv, device):
        return pltpu.make_async_remote_copy(
            src_ref=src, dst_ref=dst, send_sem=send, recv_sem=recv, device_id=device, device_id_type=MESH
        )

    def start(self, copy):
        copy.start()
        self.started.append(copy)

    def finish(self):
        for copy in self.started:
            copy.wait_send()


def chain(ids, live):
    slots = ids.shape[1]
    t = lax.broadcasted_iota(jnp.int32, (slots, slots), 0)
    s = lax.broadcasted_iota(jnp.int32, (slots, slots), 1)
    along = jnp.broadcast_to(ids, (slots, slots))
    down = jnp.sum(jnp.where(t == s, along, 0), axis=1, keepdims=True)
    used = t < live
    prev = jnp.max(jnp.where((down == along) & (t < s) & used, t, -1), axis=0, keepdims=True)
    last = jnp.max(jnp.where((down == s) & used, t, -1), axis=0, keepdims=True)
    return jnp.where(prev < 0, slots, prev), jnp.where(last < 0, slots, last)


def layer_kernel(
    scale,
    rows_h, cols_h, counts, feats_h, vals_h, dst_h, cot_h, w_self_h, w_neigh_h,
    out_h, w_out_h, source_h,
    rows, cols, tables, table, out, w_out, source, feats, vals, dst, cot, w_self, w_neigh, sums, grads,
    c_send, got_c, x_send, got_x, z_send, got_z,
    h_send, got_h, y_send, got_y,
    w_full, w_c, w_half, w_send, got_w, w_mine, w_rows,
    load_sem, table_sem, store_sem,
    c_s, c_r, x_s, x_r, z_s, z_r, h_s, h_r, y_s, y_r,
    gz_s, gz_r, gx_s, gx_r, gc_s, gc_r,
    wc_s, wc_r, wz_s, wz_r, wr_s, wr_r, wg_s, wg_r, wl_s, wl_r,
):
    remote = Copies()
    row, col = lax.axis_index("row"), lax.axis_index("col")
    z, x, k = col // 4, (col // 2) % 2, col % 2
    y, h = row // 2, row % 2
    slots = vals.shape[0]
    quarter = slots // 4

    def at_col(zz, xx, kk):
        return (row, (zz % N) * 4 + xx * 2 + kk)

    def at_row(yy, hh):
        return ((yy % N) * 2 + hh, col)

    mine = k * 2 * N + x * N
    me = mine + z
    sibling, beside, across = at_col(z, x, 1 - k), at_col(z, 1 - x, k), at_row(y, 1 - h)

    def near(i):
        return at_col(z + i % N, (x + i // N) % 2, k)

    def far(i):
        return at_row(y + i % N, (h + i // N) % 2)

    barrier = pltpu.get_barrier_semaphore()

    def wz_copy(i):
        ref = w_send.at[((x + i // N) % 2) * N + (z + i) % N]
        return remote(ref, got_w.at[i], wz_s.at[i], wz_r.at[i], near(i))

    def wr_copy(i):
        return remote(w_mine, w_rows.at[row], wr_s.at[i], wr_r.at[i], far(i))

    def wg_copy(i):
        return remote(w_out.at[me], w_out.at[me], wg_s.at[i], wg_r.at[i], near(i))

    def greet(i, c):
        pl.semaphore_signal(barrier, inc=1, device_id=near(i), device_id_type=MESH)
        pl.semaphore_signal(barrier, inc=1, device_id=far(i), device_id_type=MESH)
        return c

    pl.semaphore_signal(barrier, inc=1, device_id=sibling, device_id_type=MESH)
    lax.fori_loop(1, 2 * N, greet, 0)

    loads = []
    for i, (src, dest) in enumerate(((rows_h, rows), (cols_h, cols), (feats_h, feats))):
        loads.append(pltpu.make_async_copy(src, dest, load_sem.at[i]))
    for i in range(4):
        part = pl.ds(i * quarter, quarter)
        loads.append(pltpu.make_async_copy(vals_h.at[part], vals.at[part], load_sem.at[3 + i]))
    for i, (src, dest) in enumerate(((dst_h, dst), (w_self_h, w_self), (w_neigh_h, w_neigh), (cot_h, cot))):
        loads.append(pltpu.make_async_copy(src, dest, load_sem.at[7 + i]))
    for load in loads:
        load.start()

    sums[slots] = jnp.zeros_like(sums[slots])
    tables[...] = jnp.zeros_like(tables)
    for load in loads[:2]:
        load.wait()
    r, c = rows[...], cols[...]
    row_prev, row_last = chain(r, counts[0, 0])
    col_prev, col_last = chain(c, counts[0, 0])
    at = (r % 2) * (2 * N) + ((r // 2) % 2) * N + r // 4
    for i, line in enumerate((row_prev, row_last, col_prev, col_last, c, at)):
        tables[pl.ds(i, 1), pl.ds(0, slots)] = line
    to_scalars = pltpu.make_async_copy(tables, table, table_sem)
    to_scalars.start()
    to_scalars.wait()

    loads[2].wait()
    for s in range(slots):
        if s % quarter == 0:
            loads[3 + s // quarter].wait()
        sums[s] = sums[table[0, s]] + jnp.dot(vals[s], feats[table[4, s]], preferred_element_type=F32)

    def partial(zz, xx, kk):
        return sums[table[1, (zz % N) * 4 + xx * 2 + kk]]

    pl.semaphore_wait(barrier, 4 * N - 1)

    def c_copy(i):
        return remote(c_send.at[i], got_c.at[i], c_s.at[i], c_r.at[i], sibling)

    for i in range(2 * N):
        c_send[i] = partial(z + OFFSETS[i % N], 1 - x if i < N else x, 1 - k).astype(BF16)
        remote.start(c_copy(i))

    def x_copy(i):
        return remote(x_send.at[i], got_x.at[i], x_s.at[i], x_r.at[i], beside)

    for i in range(N):
        own = partial(z + OFFSETS[i], 1 - x, k)
        c_copy(i).wait_recv()
        x_send[i] = (own + got_c[i].astype(F32)).astype(BF16)
        remote.start(x_copy(i))

    for load in loads[7:]:
        load.wait()
    pre_self = jnp.dot(dst[...], w_self[...], preferred_element_type=F32)

    def col_piece(i):
        own = partial(z + OFFSETS[i], x, k)
        c_copy(N + i).wait_recv()
        own += got_c[N + i].astype(F32)
        x_copy(i).wait_recv()
        return own + got_x[i].astype(F32)

    def z_copy(i):
        return remote(z_send.at[i], got_z.at[i], z_s.at[i], z_r.at[i], at_col(z + OFFSETS[i], x, k))

    for i in range(N - 1):
        z_send[i] = col_piece(i).astype(BF16)
        remote.start(z_copy(i))
    total = col_piece(N - 1)
    for i in range(N - 1):
        z_copy(i).wait_recv()
        total += got_z[i].astype(F32)
    agg = total.astype(BF16)

    pre = pre_self + jnp.dot(agg, w_neigh[...], preferred_element_type=F32)
    sig = jax.nn.sigmoid(pre)
    gpre = (cot[...].astype(F32) * sig * (1.0 + pre * (1.0 - sig))).astype(BF16)
    grads[me] = lax.dot_general(
        gpre, w_neigh[...], (((1,), (1,)), ((), ())), preferred_element_type=F32
    ).astype(BF16)

    def gz_copy(i):
        ref = grads.at[me]
        return remote(ref, ref, gz_s.at[i], gz_r.at[i], at_col(z + SPREAD[i], x, k))

    def gx_copy(off):
        ref = grads.at[mine + (z + N - off) % N]
        return remote(ref, ref, gx_s.at[off], gx_r.at[off], beside)

    def gc_copy(other, off):
        ref = grads.at[k * 2 * N + ((x + other) % 2) * N + (z + N - off) % N]
        return remote(ref, ref, gc_s.at[other * N + off], gc_r.at[other * N + off], sibling)

    for i in range(N - 1):
        remote.start(gz_copy(i))
    remote.start(gx_copy(0))
    remote.start(gc_copy(0, 0))
    out[...] = (pre * sig).astype(BF16)
    stores = [pltpu.make_async_copy(out, out_h, store_sem.at[0])]
    stores[0].start()

    feat = dst.shape[1]
    pieces, wide, hid = w_full.shape
    half = pieces // 2
    for base, left in ((0, dst[...]), (1, agg)):
        dw = lax.dot_general(left, gpre, (((0,), (0,)), ((), ())), preferred_element_type=F32)
        w_full[pl.ds(base * half, half)] = dw.reshape(half, wide, hid)
    wc_copy = remote(w_full.at[pl.ds((1 - k) * half, half)], w_c, wc_s, wc_r, sibling)
    remote.start(wc_copy)

    def from_beside(off):
        gx_copy(off).wait_recv()
        remote.start(gc_copy(1, off))

    wc_copy.wait_recv()
    w_half[...] = w_full[pl.ds(k * half, half)] + w_c[...]
    w_send[...] = w_half[...].astype(BF16)
    for i in range(1, 2 * N):
        remote.start(wz_copy(i))
    for i, off in enumerate(SPREAD):
        gz_copy(i).wait_recv()
        remote.start(gx_copy(off))
        remote.start(gc_copy(0, off))
        if i == 3:
            from_beside(0)

    total = w_half[x * N + z]
    for i in range(1, 2 * N):
        wz_copy(i).wait_recv()
        total += got_w[i].astype(F32)
    w_mine[...] = total
    w_rows[row] = total
    for i in range(1, 2 * N):
        remote.start(wr_copy(i))
    for off in SPREAD:
        from_beside(off)
    for i in range(2 * N):
        gc_copy(i // N, i % N).wait_recv()

    for s in range(slots):
        sums[s] = sums[table[2, s]] + lax.dot_general(
            vals[s], grads[table[5, s]], (((0,), (0,)), ((), ())), preferred_element_type=F32
        )

    def source_partial(yy, hh):
        return sums[table[3, (yy % N) * 2 + hh]]

    def h_copy(i):
        return remote(h_send.at[i], got_h.at[i], h_s.at[i], h_r.at[i], across)

    for i in range(N):
        h_send[i] = source_partial(y + OFFSETS[i], 1 - h).astype(BF16)
        remote.start(h_copy(i))

    for i in range(1, 2 * N):
        wr_copy(i).wait_recv()
    total = w_rows[0]
    for i in range(1, 2 * N):
        total += w_rows[i]
    w_out[me] = total * scale
    for i in range(1, 2 * N):
        remote.start(wg_copy(i))

    def y_copy(i):
        return remote(y_send.at[i], got_y.at[i], y_s.at[i], y_r.at[i], at_row(y + OFFSETS[i], h))

    def row_piece(i):
        own = source_partial(y + OFFSETS[i], h)
        h_copy(i).wait_recv()
        return own + got_h[i].astype(F32)

    for i in range(N - 1):
        y_send[i] = row_piece(i).astype(BF16)
        remote.start(y_copy(i))

    for i in range(1, 2 * N):
        wg_copy(i).wait_recv()
    ref = w_out.at[pl.ds(k * half, half)]
    wl_copy = remote(ref, ref, wl_s, wl_r, sibling)
    remote.start(wl_copy)

    total = row_piece(N - 1)
    for i in range(N - 1):
        y_copy(i).wait_recv()
        total += got_y[i].astype(F32)
    source[...] = total
    stores.append(pltpu.make_async_copy(source, source_h, store_sem.at[1]))
    stores[1].start()
    wl_copy.wait_recv()
    stores.append(pltpu.make_async_copy(w_out, w_out_h, store_sem.at[2]))
    stores[2].start()
    remote.finish()
    for store in stores:
        store.wait()


def layer(scale, rows, cols, counts, feats, vals, dst, cot, w_self, w_neigh):
    slots, block, _ = vals.shape
    width = feats.shape[-1]
    hid = w_self.shape[1]
    wide = 2 * width // (4 * N)
    results = (
        jax.ShapeDtypeStruct((block, hid), BF16),
        jax.ShapeDtypeStruct((4 * N, wide, hid), F32),
        jax.ShapeDtypeStruct((block, width), F32),
    )

    def like(a):
        return pltpu.VMEM(a.shape, a.dtype)

    def blocks(n, kind=BF16):
        return pltpu.VMEM((n, block, width), kind)

    def slabs(n, kind=F32):
        return pltpu.VMEM((n, wide, hid), kind)

    return pl.pallas_call(
        functools.partial(layer_kernel, scale),
        out_shape=results,
        in_specs=[HBM, HBM, SMEM] + [HBM] * 6,
        out_specs=(HBM,) * 3,
        scratch_shapes=[
            like(rows), like(cols), pltpu.VMEM((8, 128), jnp.int32), pltpu.SMEM((8, 128), jnp.int32),
            *map(like, results), like(feats), like(vals), like(dst), like(cot), like(w_self), like(w_neigh),
            blocks(slots + 1, F32), blocks(4 * N),
            blocks(2 * N), blocks(2 * N), blocks(N), blocks(N), blocks(N - 1), blocks(N - 1),
            blocks(N), blocks(N), blocks(N - 1), blocks(N - 1),
            slabs(4 * N), slabs(2 * N), slabs(2 * N), slabs(2 * N, BF16), slabs(2 * N, BF16),
            pltpu.VMEM((wide, hid), F32), slabs(2 * N),
            DMA((11,)), DMA, DMA((3,)),
            DMA((2 * N,)), DMA((2 * N,)), DMA((N,)), DMA((N,)), DMA((N,)), DMA((N,)),
            DMA((N,)), DMA((N,)), DMA((N,)), DMA((N,)),
            DMA((N,)), DMA((N,)), DMA((N,)), DMA((N,)), DMA((2 * N,)), DMA((2 * N,)),
            DMA, DMA, DMA((2 * N,)), DMA((2 * N,)), DMA((2 * N,)), DMA((2 * N,)), DMA((2 * N,)), DMA((2 * N,)),
            DMA, DMA,
        ],
        compiler_params=pltpu.CompilerParams(
            collective_id=0, has_side_effects=True, vmem_limit_bytes=60 * 1024 * 1024
        ),
    )(rows, cols, counts, feats, vals, dst, cot, w_self, w_neigh)


def hand_kernel(out_h, w_h, source_h, out, w_self, w_neigh, source, out_v, w_v, source_v, sem):
    half = w_self.shape[0]
    low, high = pl.ds(0, half), pl.ds(half, half)
    ways = (
        (w_h.at[low], w_v.at[low], w_self),
        (w_h.at[high], w_v.at[high], w_neigh),
        (out_h, out_v, out),
        (source_h, source_v, source),
    )
    loads = [pltpu.make_async_copy(src, via, sem.at[0, i]) for i, (src, via, _) in enumerate(ways)]
    stores = [pltpu.make_async_copy(via, dest, sem.at[1, i]) for i, (_, via, dest) in enumerate(ways)]
    for load in loads:
        load.start()
    for load, store in zip(loads, stores):
        load.wait()
        store.start()
    for store in stores:
        store.wait()


def hand(out, w_all, source):
    pieces, wide, hid = w_all.shape
    grad = jax.ShapeDtypeStruct((pieces // 2, wide, hid), F32)
    return pl.pallas_call(
        hand_kernel,
        out_shape=(jax.ShapeDtypeStruct(out.shape, BF16), grad, grad, jax.ShapeDtypeStruct(source.shape, F32)),
        in_specs=[HBM] * 3,
        out_specs=(HBM,) * 4,
        scratch_shapes=[*(pltpu.VMEM(a.shape, a.dtype) for a in (out, w_all, source)), DMA((2, 4))],
        compiler_params=pltpu.CompilerParams(vmem_limit_bytes=60 * 1024 * 1024),
    )(out, w_all, source)


def per_device(features, dst_features, w_self, w_neigh, cotangent, block_values, block_rows, block_cols, block_counts):
    block = block_values.shape[-1]
    width = features.shape[-1]
    nodes = dst_features.shape[0] * lax.axis_size("row") * lax.axis_size("col")
    results = layer(
        1.0 / math.sqrt(nodes), block_rows[0], block_cols[0], block_counts, features.reshape(-1, block, width),
        block_values[0, 0], dst_features, cotangent, w_self, w_neigh,
    )
    out, grad_self, grad_neigh, source = hand(*results)
    return out, grad_self.reshape(width, -1), grad_neigh.reshape(width, -1), source[None]


def solution(mesh):
    placed = (
        P("col", None, None),
        P(("row", "col"), None),
        P(),
        P(),
        P(("row", "col"), None),
        P("row", "col", None, None, None),
        P("row", "col", None),
        P("row", "col", None),
        P("row", "col"),
    )
    return jax.shard_map(
        per_device,
        mesh=mesh,
        in_specs=placed,
        out_specs=(P(("row", "col"), None), P(), P(), P("col", "row", None)),
        check_vma=False,
    )
```

```python
import functools
import math

import jax
import jax.numpy as jnp
from jax import lax
from jax.experimental import pallas as pl
from jax.experimental.pallas import tpu as pltpu
from jax.sharding import PartitionSpec as P

BF16 = jnp.bfloat16
F32 = jnp.float32
MESH = pl.DeviceIdType.MESH
N = 8
OFFSETS = (4, 3, 5, 2, 6, 1, 7, 0)
SPREAD = (1, 7, 2, 6, 3, 5, 4)
SMEM = pl.BlockSpec(memory_space=pltpu.SMEM)
HBM = pl.BlockSpec(memory_space=pltpu.HBM)
DMA = pltpu.SemaphoreType.DMA


class Copies:
    def __init__(self):
        self.started = []

    def __call__(self, src, dst, send, recv, device):
        return pltpu.make_async_remote_copy(
            src_ref=src, dst_ref=dst, send_sem=send, recv_sem=recv, device_id=device, device_id_type=MESH
        )

    def start(self, copy):
        copy.start()
        self.started.append(copy)

    def finish(self):
        for copy in self.started:
            copy.wait_send()
        self.started = []


def chain(ids, live):
    slots = ids.shape[1]
    t = lax.broadcasted_iota(jnp.int32, (slots, slots), 0)
    s = lax.broadcasted_iota(jnp.int32, (slots, slots), 1)
    along = jnp.broadcast_to(ids, (slots, slots))
    down = jnp.sum(jnp.where(t == s, along, 0), axis=1, keepdims=True)
    used = t < live
    prev = jnp.max(jnp.where((down == along) & (t < s) & used, t, -1), axis=0, keepdims=True)
    last = jnp.max(jnp.where((down == s) & used, t, -1), axis=0, keepdims=True)
    return jnp.where(prev < 0, slots, prev), jnp.where(last < 0, slots, last)


def layer_kernel(
    scale,
    rows_h, cols_h, counts, feats_h, vals_h, dst_h, cot_h, w_self_h, w_neigh_h,
    out_h, w_out_h, own_h, got_y,
    rows, cols, tables, table, out, w_out, kept, feats, vals, dst, cot, w_self, w_neigh, sums, grads,
    c_send, got_c, x_send, got_x, z_send, got_z, agg, pre_self, gpre,
    h_send, got_h, y_send,
    w_full, w_c, w_half, w_send, got_w, w_mine, w_rows,
    load_sem, table_sem, store_sem,
    c_s, c_r, x_s, x_r, z_s, z_r, h_s, h_r, y_s, y_r,
    gz_s, gz_r, gx_s, gx_r, gc_s, gc_r,
    wc_s, wc_r, wz_s, wz_r, wr_s, wr_r, wg_s, wg_r, wl_s, wl_r,
):
    remote = Copies()
    row, col = lax.axis_index("row"), lax.axis_index("col")
    z, x, k = col // 4, (col // 2) % 2, col % 2
    y, h = row // 2, row % 2
    slots = vals.shape[0]
    quarter = slots // 4
    tall = dst.shape[0] // 2
    halves = (pl.ds(0, tall), pl.ds(tall, tall))

    def at_col(zz, xx, kk):
        return (row, (zz % N) * 4 + xx * 2 + kk)

    def at_row(yy, hh):
        return ((yy % N) * 2 + hh, col)

    mine = k * 2 * N + x * N
    me = mine + z
    sibling, beside, across = at_col(z, x, 1 - k), at_col(z, 1 - x, k), at_row(y, 1 - h)

    def near(i):
        return at_col(z + i % N, (x + i // N) % 2, k)

    def far(i):
        return at_row(y + i % N, (h + i // N) % 2)

    loads = []
    for i, (src, dest) in enumerate(((rows_h, rows), (cols_h, cols), (feats_h, feats))):
        loads.append(pltpu.make_async_copy(src, dest, load_sem.at[i]))
    for i in range(4):
        part = pl.ds(i * quarter, quarter)
        loads.append(pltpu.make_async_copy(vals_h.at[part], vals.at[part], load_sem.at[3 + i]))
    for i, (src, dest) in enumerate(((dst_h, dst), (w_self_h, w_self), (w_neigh_h, w_neigh), (cot_h, cot))):
        loads.append(pltpu.make_async_copy(src, dest, load_sem.at[7 + i]))
    for load in loads:
        load.start()

    barrier = pltpu.get_barrier_semaphore()

    def wz_copy(i):
        ref = w_send.at[((x + i // N) % 2) * N + (z + i) % N]
        return remote(ref, got_w.at[i], wz_s.at[i], wz_r.at[i], near(i))

    def wr_copy(i):
        return remote(w_mine, w_rows.at[row], wr_s.at[i], wr_r.at[i], far(i))

    def wg_copy(i):
        return remote(w_out.at[me], w_out.at[me], wg_s.at[i], wg_r.at[i], near(i))

    def greet(i, c):
        pl.semaphore_signal(barrier, inc=1, device_id=near(i), device_id_type=MESH)
        pl.semaphore_signal(barrier, inc=1, device_id=far(i), device_id_type=MESH)
        return c

    pl.semaphore_signal(barrier, inc=1, device_id=sibling, device_id_type=MESH)
    lax.fori_loop(1, 2 * N, greet, 0)

    sums[slots] = jnp.zeros_like(sums[slots])
    tables[...] = jnp.zeros_like(tables)
    for load in loads[:2]:
        load.wait()
    r, c = rows[...], cols[...]
    row_prev, row_last = chain(r, counts[0, 0])
    col_prev, col_last = chain(c, counts[0, 0])
    at = (r % 2) * (2 * N) + ((r // 2) % 2) * N + r // 4
    for i, line in enumerate((row_prev, row_last, col_prev, col_last, c, at)):
        tables[pl.ds(i, 1), pl.ds(0, slots)] = line
    to_scalars = pltpu.make_async_copy(tables, table, table_sem)
    to_scalars.start()
    to_scalars.wait()

    loads[2].wait()
    for s in range(slots):
        if s % quarter == 0:
            loads[3 + s // quarter].wait()
        sums[s] = sums[table[0, s]] + jnp.dot(vals[s], feats[table[4, s]], preferred_element_type=F32)

    def partial(zz, xx, kk):
        return sums[table[1, (zz % N) * 4 + xx * 2 + kk]]

    pl.semaphore_wait(barrier, 4 * N - 1)

    def c_copy(i):
        return remote(c_send.at[i], got_c.at[i], c_s.at[i], c_r.at[i], sibling)

    def c_step(i):
        c_send[i] = partial(z + OFFSETS[i % N], 1 - x if i < N else x, 1 - k).astype(BF16)
        remote.start(c_copy(i))

    for i in range(N):
        c_step(i)

    def x_copy(p, i):
        return remote(
            x_send.at[i, halves[p]], got_x.at[i, halves[p]], x_s.at[p, i], x_r.at[p, i], beside
        )

    for i in range(N):
        own = partial(z + OFFSETS[i], 1 - x, k)
        c_copy(i).wait_recv()
        x_send[i] = (own + got_c[i].astype(F32)).astype(BF16)
        remote.start(x_copy(0, i))
        c_step(N + i)
    for i in range(N):
        remote.start(x_copy(1, i))

    for load in loads[7:]:
        load.wait()
    pre_self[...] = jnp.dot(dst[...], w_self[...], preferred_element_type=F32)

    def col_piece(p, i):
        own = partial(z + OFFSETS[i], x, k)[p * tall : (p + 1) * tall]
        if p == 0:
            c_copy(N + i).wait_recv()
        own += got_c[N + i, halves[p]].astype(F32)
        x_copy(p, i).wait_recv()
        return own + got_x[i, halves[p]].astype(F32)

    def z_copy(p, i):
        return remote(
            z_send.at[i, halves[p]], got_z.at[i, halves[p]], z_s.at[p, i], z_r.at[p, i], at_col(z + OFFSETS[i], x, k)
        )

    def gz_copy(p, i):
        ref = grads.at[me, halves[p]]
        return remote(ref, ref, gz_s.at[p, i], gz_r.at[p, i], at_col(z + SPREAD[i], x, k))

    def gx_copy(p, off):
        ref = grads.at[mine + (z + N - off) % N, halves[p]]
        return remote(ref, ref, gx_s.at[p, off], gx_r.at[p, off], beside)

    def gc_copy(other, off):
        ref = grads.at[k * 2 * N + ((x + other) % 2) * N + (z + N - off) % N]
        return remote(ref, ref, gc_s.at[other * N + off], gc_r.at[other * N + off], sibling)

    totals = []
    for p in range(2):
        for i in range(N - 1):
            z_send[i, halves[p]] = col_piece(p, i).astype(BF16)
            remote.start(z_copy(p, i))
        totals.append(col_piece(p, N - 1))

    for p, rows_p in enumerate(halves):
        total = totals[p]
        for i in range(N - 1):
            z_copy(p, i).wait_recv()
            total += got_z[i, rows_p].astype(F32)
        agg[rows_p] = total.astype(BF16)
        pre = pre_self[rows_p] + jnp.dot(agg[rows_p], w_neigh[...], preferred_element_type=F32)
        sig = jax.nn.sigmoid(pre)
        gpre[rows_p] = (cot[rows_p].astype(F32) * sig * (1.0 + pre * (1.0 - sig))).astype(BF16)
        grads[me, rows_p] = lax.dot_general(
            gpre[rows_p], w_neigh[...], (((1,), (1,)), ((), ())), preferred_element_type=F32
        ).astype(BF16)
        for i in range(N - 1):
            remote.start(gz_copy(p, i))
        remote.start(gx_copy(p, 0))
        out[rows_p] = (pre * sig).astype(BF16)
    remote.start(gc_copy(0, 0))
    stores = [pltpu.make_async_copy(out, out_h, store_sem.at[0])]
    stores[0].start()

    feat = dst.shape[1]
    pieces, wide, hid = w_full.shape
    half = pieces // 2
    for base, left in ((0, dst), (1, agg)):
        dw = lax.dot_general(left[...], gpre[...], (((0,), (0,)), ((), ())), preferred_element_type=F32)
        w_full[pl.ds(base * half, half)] = dw.reshape(half, wide, hid)
    wc_copy = remote(w_full.at[pl.ds((1 - k) * half, half)], w_c, wc_s, wc_r, sibling)
    remote.start(wc_copy)

    def from_beside(off):
        gx_copy(0, off).wait_recv()
        gx_copy(1, off).wait_recv()
        remote.start(gc_copy(1, off))

    for i, off in enumerate(SPREAD):
        gz_copy(0, i).wait_recv()
        remote.start(gx_copy(0, off))
    wc_copy.wait_recv()
    w_half[...] = w_full[pl.ds(k * half, half)] + w_c[...]
    w_send[...] = w_half[...].astype(BF16)
    for i in range(1, 2 * N):
        remote.start(wz_copy(i))
    for i, off in enumerate(SPREAD):
        gz_copy(1, i).wait_recv()
        remote.start(gx_copy(1, off))
        remote.start(gc_copy(0, off))
        if i == 3:
            from_beside(0)

    total = w_half[x * N + z]
    for i in range(1, 2 * N):
        wz_copy(i).wait_recv()
        total += got_w[i].astype(F32)
    w_mine[...] = total
    w_rows[row] = total
    for i in range(1, 2 * N):
        remote.start(wr_copy(i))
    for off in SPREAD:
        from_beside(off)
    for i in range(2 * N):
        gc_copy(i // N, i % N).wait_recv()

    for s in range(slots):
        sums[s] = sums[table[2, s]] + lax.dot_general(
            vals[s], grads[table[5, s]], (((0,), (0,)), ((), ())), preferred_element_type=F32
        )

    def source_partial(yy, hh):
        return sums[table[3, (yy % N) * 2 + hh]]

    def h_copy(i):
        return remote(h_send.at[i], got_h.at[i], h_s.at[i], h_r.at[i], across)

    for i in range(N):
        h_send[i] = source_partial(y + OFFSETS[i], 1 - h).astype(BF16)
        remote.start(h_copy(i))

    for i in range(1, 2 * N):
        wr_copy(i).wait_recv()
    total = w_rows[0]
    for i in range(1, 2 * N):
        total += w_rows[i]
    w_out[me] = total * scale
    for i in range(1, 2 * N):
        remote.start(wg_copy(i))

    def y_copy(i):
        return remote(y_send.at[i], got_y.at[i], y_s.at[i], y_r.at[i], at_row(y + OFFSETS[i], h))

    def row_piece(i):
        own = source_partial(y + OFFSETS[i], h)
        h_copy(i).wait_recv()
        return own + got_h[i].astype(F32)

    for i in range(N - 1):
        y_send[i] = row_piece(i).astype(BF16)
        remote.start(y_copy(i))

    kept[...] = row_piece(N - 1)
    stores.append(pltpu.make_async_copy(kept, own_h, store_sem.at[1]))
    stores[1].start()
    for i in range(1, 2 * N):
        wg_copy(i).wait_recv()
    ref = pl.ds(k * half, half)
    wl_copy = remote(w_out.at[ref], w_out_h.at[ref], wl_s, wl_r, sibling)
    remote.start(wl_copy)
    stores.append(pltpu.make_async_copy(w_out.at[ref], w_out_h.at[ref], store_sem.at[2]))
    stores[2].start()
    remote.finish()
    for store in stores:
        store.wait()
    for i in range(N - 1):
        y_copy(i).wait_recv()
    wl_copy.wait_recv()


def layer(scale, rows, cols, counts, feats, vals, dst, cot, w_self, w_neigh):
    slots, block, _ = vals.shape
    width = feats.shape[-1]
    hid = w_self.shape[1]
    wide = 2 * width // (4 * N)
    results = (
        jax.ShapeDtypeStruct((block, hid), BF16),
        jax.ShapeDtypeStruct((4 * N, wide, hid), F32),
        jax.ShapeDtypeStruct((block, width), F32),
        jax.ShapeDtypeStruct((N - 1, block, width), BF16),
    )

    def like(a):
        return pltpu.VMEM(a.shape, a.dtype)

    def blocks(n, kind=BF16):
        return pltpu.VMEM((n, block, width), kind)

    def slabs(n, kind=F32):
        return pltpu.VMEM((n, wide, hid), kind)

    return pl.pallas_call(
        functools.partial(layer_kernel, scale),
        out_shape=results,
        in_specs=[HBM, HBM, SMEM] + [HBM] * 6,
        out_specs=(HBM,) * 4,
        scratch_shapes=[
            like(rows), like(cols), pltpu.VMEM((8, 128), jnp.int32), pltpu.SMEM((8, 128), jnp.int32),
            *map(like, results[:3]), like(feats), like(vals), like(dst), like(cot), like(w_self), like(w_neigh),
            blocks(slots + 1, F32), blocks(4 * N),
            blocks(2 * N), blocks(2 * N), blocks(N), blocks(N), blocks(N - 1), blocks(N - 1),
            like(dst), pltpu.VMEM(cot.shape, F32), like(cot),
            blocks(N), blocks(N), blocks(N - 1),
            slabs(4 * N), slabs(2 * N), slabs(2 * N), slabs(2 * N, BF16), slabs(2 * N, BF16),
            pltpu.VMEM((wide, hid), F32), slabs(2 * N),
            DMA((11,)), DMA, DMA((3,)),
            DMA((2 * N,)), DMA((2 * N,)), DMA((2, N)), DMA((2, N)), DMA((2, N)), DMA((2, N)),
            DMA((N,)), DMA((N,)), DMA((N,)), DMA((N,)),
            DMA((2, N)), DMA((2, N)), DMA((2, N)), DMA((2, N)), DMA((2 * N,)), DMA((2 * N,)),
            DMA, DMA, DMA((2 * N,)), DMA((2 * N,)), DMA((2 * N,)), DMA((2 * N,)), DMA((2 * N,)), DMA((2 * N,)),
            DMA, DMA,
        ],
        compiler_params=pltpu.CompilerParams(
            collective_id=0, has_side_effects=True, vmem_limit_bytes=60 * 1024 * 1024
        ),
    )(rows, cols, counts, feats, vals, dst, cot, w_self, w_neigh)


def hand_kernel(out_h, w_h, own_h, parts_h, out, w_self, w_neigh, source, out_v, w_v, own_v, parts_v, sem):
    half = w_self.shape[0]
    low, high = pl.ds(0, half), pl.ds(half, half)
    ways = (
        (parts_h, parts_v, None),
        (own_h, own_v, source),
        (w_h.at[low], w_v.at[low], w_self),
        (w_h.at[high], w_v.at[high], w_neigh),
        (out_h, out_v, out),
    )
    loads = [pltpu.make_async_copy(src, via, sem.at[0, i]) for i, (src, via, _) in enumerate(ways)]
    stores = [pltpu.make_async_copy(via, dest, sem.at[1, i]) for i, (_, via, dest) in enumerate(ways) if dest is not None]
    for load in loads:
        load.start()
    for load in loads[:2]:
        load.wait()
    total = own_v[...]
    for i in range(parts_v.shape[0]):
        total += parts_v[i].astype(F32)
    own_v[...] = total
    stores[0].start()
    for load, store in zip(loads[2:], stores[1:]):
        load.wait()
        store.start()
    for store in stores:
        store.wait()


def hand(out, w_all, own, parts):
    pieces, wide, hid = w_all.shape
    grad = jax.ShapeDtypeStruct((pieces // 2, wide, hid), F32)
    return pl.pallas_call(
        hand_kernel,
        out_shape=(jax.ShapeDtypeStruct(out.shape, BF16), grad, grad, jax.ShapeDtypeStruct(own.shape, F32)),
        in_specs=[HBM] * 4,
        out_specs=(HBM,) * 4,
        scratch_shapes=[*(pltpu.VMEM(a.shape, a.dtype) for a in (out, w_all, own, parts)), DMA((2, 5))],
        compiler_params=pltpu.CompilerParams(vmem_limit_bytes=60 * 1024 * 1024),
    )(out, w_all, own, parts)


def per_device(features, dst_features, w_self, w_neigh, cotangent, block_values, block_rows, block_cols, block_counts):
    block = block_values.shape[-1]
    width = features.shape[-1]
    nodes = dst_features.shape[0] * lax.axis_size("row") * lax.axis_size("col")
    results = layer(
        1.0 / math.sqrt(nodes), block_rows[0], block_cols[0], block_counts, features.reshape(-1, block, width),
        block_values[0, 0], dst_features, cotangent, w_self, w_neigh,
    )
    out, grad_self, grad_neigh, source = hand(*results)
    return out, grad_self.reshape(width, -1), grad_neigh.reshape(width, -1), source[None]


def solution(mesh):
    placed = (
        P("col", None, None),
        P(("row", "col"), None),
        P(),
        P(),
        P(("row", "col"), None),
        P("row", "col", None, None, None),
        P("row", "col", None),
        P("row", "col", None),
        P("row", "col"),
    )
    return jax.shard_map(
        per_device,
        mesh=mesh,
        in_specs=placed,
        out_specs=(P(("row", "col"), None), P(), P(), P("col", "row", None)),
        check_vma=False,
    )
```

```python
import functools
import math

import jax
import jax.numpy as jnp
from jax import lax
from jax.experimental import pallas as pl
from jax.experimental.pallas import tpu as pltpu
from jax.sharding import PartitionSpec as P

BF16 = jnp.bfloat16
F32 = jnp.float32
MESH = pl.DeviceIdType.MESH
N = 8
SHARES = (64, 64)
PARTS = len(SHARES)
OFFSETS = (4, 3, 5, 2, 6, 1, 7, 0)
GREETED = (12, 4, 11, 13, 3, 5, 10, 14, 2, 6, 9, 15, 1, 7, 8)
SPREAD = (1, 7, 2, 6, 3, 5, 4)
SMEM = pl.BlockSpec(memory_space=pltpu.SMEM)
HBM = pl.BlockSpec(memory_space=pltpu.HBM)
DMA = pltpu.SemaphoreType.DMA


class Copies:
    def __init__(self):
        self.started = []

    def __call__(self, src, dst, send, recv, device):
        return pltpu.make_async_remote_copy(
            src_ref=src, dst_ref=dst, send_sem=send, recv_sem=recv, device_id=device, device_id_type=MESH
        )

    def start(self, copy):
        copy.start()
        self.started.append(copy)

    def finish(self):
        for copy in self.started:
            copy.wait_send()
        self.started = []


def chain(ids, live):
    slots = ids.shape[1]
    t = lax.broadcasted_iota(jnp.int32, (slots, slots), 0)
    s = lax.broadcasted_iota(jnp.int32, (slots, slots), 1)
    along = jnp.broadcast_to(ids, (slots, slots))
    down = jnp.sum(jnp.where(t == s, along, 0), axis=1, keepdims=True)
    used = t < live
    prev = jnp.max(jnp.where((down == along) & (t < s) & used, t, -1), axis=0, keepdims=True)
    last = jnp.max(jnp.where((down == s) & used, t, -1), axis=0, keepdims=True)
    return jnp.where(prev < 0, slots, prev), jnp.where(last < 0, slots, last)


def layer_kernel(
    scale,
    rows_h, cols_h, counts, feats_h, vals_h, dst_h, cot_h, w_self_h, w_neigh_h,
    out_h, w_out_h, own_h, got_y,
    rows, cols, tables, table, out, w_out, kept, feats, vals, dst, cot, w_self, w_neigh, sums, grads,
    c_send, got_c, x_send, got_x, z_send, got_z, agg, pre_self, gpre,
    h_send, got_h, y_send,
    w_full, w_c, w_half, w_send, got_w, w_mine, w_rows,
    load_sem, table_sem, store_sem,
    c_s, c_r, x_s, x_r, z_s, z_r, h_s, h_r, y_s, y_r,
    gz_s, gz_r, gx_s, gx_r, gc_s, gc_r,
    wc_s, wc_r, wz_s, wz_r, wr_s, wr_r, wg_s, wg_r, wl_s, wl_r,
):
    remote = Copies()
    row, col = lax.axis_index("row"), lax.axis_index("col")
    z, x, k = col // 4, (col // 2) % 2, col % 2
    y, h = row // 2, row % 2
    slots = vals.shape[0]
    quarter = slots // 4
    shares = [pl.ds(sum(SHARES[:p]), tall) for p, tall in enumerate(SHARES)]

    def at_col(zz, xx, kk):
        return (row, (zz % N) * 4 + xx * 2 + kk)

    def at_row(yy, hh):
        return ((yy % N) * 2 + hh, col)

    mine = k * 2 * N + x * N
    me = mine + z
    sibling, beside, across = at_col(z, x, 1 - k), at_col(z, 1 - x, k), at_row(y, 1 - h)

    def near(i):
        return at_col(z + i % N, (x + i // N) % 2, k)

    def far(i):
        return at_row(y + i % N, (h + i // N) % 2)

    def wz_copy(i):
        ref = w_send.at[((x + i // N) % 2) * N + (z + i) % N]
        return remote(ref, got_w.at[i], wz_s.at[i], wz_r.at[i], near(i))

    def wr_copy(i):
        return remote(w_mine, w_rows.at[row], wr_s.at[i], wr_r.at[i], far(i))

    def wg_copy(i):
        return remote(w_out.at[me], w_out.at[me], wg_s.at[i], wg_r.at[i], near(i))

    barrier = pltpu.get_barrier_semaphore()

    def greet(device):
        pl.semaphore_signal(barrier, inc=1, device_id=device, device_id_type=MESH)

    for i in GREETED:
        greet(far(i))
        greet(near(i))
    greet(sibling)

    loads = []
    for i, (src, dest) in enumerate(((rows_h, rows), (cols_h, cols), (feats_h, feats))):
        loads.append(pltpu.make_async_copy(src, dest, load_sem.at[i]))
    for i in range(4):
        part = pl.ds(i * quarter, quarter)
        loads.append(pltpu.make_async_copy(vals_h.at[part], vals.at[part], load_sem.at[3 + i]))
    for i, (src, dest) in enumerate(((dst_h, dst), (w_self_h, w_self), (w_neigh_h, w_neigh), (cot_h, cot))):
        loads.append(pltpu.make_async_copy(src, dest, load_sem.at[7 + i]))
    for load in loads:
        load.start()

    sums[slots] = jnp.zeros_like(sums[slots])
    tables[...] = jnp.zeros_like(tables)
    for load in loads[:2]:
        load.wait()
    r, c = rows[...], cols[...]
    row_prev, row_last = chain(r, counts[0, 0])
    col_prev, col_last = chain(c, counts[0, 0])
    at = (r % 2) * (2 * N) + ((r // 2) % 2) * N + r // 4
    for i, line in enumerate((row_prev, row_last, col_prev, col_last, c, at)):
        tables[pl.ds(i, 1), pl.ds(0, slots)] = line
    to_scalars = pltpu.make_async_copy(tables, table, table_sem)
    to_scalars.start()
    to_scalars.wait()

    loads[2].wait()
    for s in range(slots):
        if s % quarter == 0:
            loads[3 + s // quarter].wait()
        sums[s] = sums[table[0, s]] + jnp.dot(vals[s], feats[table[4, s]], preferred_element_type=F32)

    def partial(zz, xx, kk):
        return sums[table[1, (zz % N) * 4 + xx * 2 + kk]]

    pl.semaphore_wait(barrier, 4 * N - 1)

    def c_copy(i):
        return remote(c_send.at[i], got_c.at[i], c_s.at[i], c_r.at[i], sibling)

    def c_step(i):
        c_send[i] = partial(z + OFFSETS[i % N], 1 - x if i < N else x, 1 - k).astype(BF16)
        remote.start(c_copy(i))

    for i in range(N):
        c_step(i)

    def x_copy(p, i):
        return remote(
            x_send.at[i, shares[p]], got_x.at[i, shares[p]], x_s.at[p, i], x_r.at[p, i], beside
        )

    for i in range(N):
        own = partial(z + OFFSETS[i], 1 - x, k)
        c_copy(i).wait_recv()
        x_send[i] = (own + got_c[i].astype(F32)).astype(BF16)
        remote.start(x_copy(0, i))
        c_step(N + i)
    for p in range(1, PARTS):
        for i in range(N):
            remote.start(x_copy(p, i))

    for load in loads[7:]:
        load.wait()
    pre_self[...] = jnp.dot(dst[...], w_self[...], preferred_element_type=F32)

    def col_piece(p, i):
        first = sum(SHARES[:p])
        own = partial(z + OFFSETS[i], x, k)[first : first + SHARES[p]]
        if p == 0:
            c_copy(N + i).wait_recv()
        own += got_c[N + i, shares[p]].astype(F32)
        x_copy(p, i).wait_recv()
        return own + got_x[i, shares[p]].astype(F32)

    def z_copy(p, i):
        return remote(
            z_send.at[i, shares[p]], got_z.at[i, shares[p]], z_s.at[p, i], z_r.at[p, i], at_col(z + OFFSETS[i], x, k)
        )

    def gz_copy(p, i):
        ref = grads.at[me, shares[p]]
        return remote(ref, ref, gz_s.at[p, i], gz_r.at[p, i], at_col(z + SPREAD[i], x, k))

    def gx_copy(p, off):
        ref = grads.at[mine + (z + N - off) % N, shares[p]]
        return remote(ref, ref, gx_s.at[p, off], gx_r.at[p, off], beside)

    def gc_copy(other, off):
        ref = grads.at[k * 2 * N + ((x + other) % 2) * N + (z + N - off) % N]
        return remote(ref, ref, gc_s.at[other * N + off], gc_r.at[other * N + off], sibling)

    totals = []
    for p in range(PARTS):
        for i in range(N - 1):
            z_send[i, shares[p]] = col_piece(p, i).astype(BF16)
            remote.start(z_copy(p, i))
        totals.append(col_piece(p, N - 1))

    for p, rows_p in enumerate(shares):
        total = totals[p]
        for i in range(N - 1):
            z_copy(p, i).wait_recv()
            total += got_z[i, rows_p].astype(F32)
        agg[rows_p] = total.astype(BF16)
        pre = pre_self[rows_p] + jnp.dot(agg[rows_p], w_neigh[...], preferred_element_type=F32)
        sig = jax.nn.sigmoid(pre)
        gpre[rows_p] = (cot[rows_p].astype(F32) * sig * (1.0 + pre * (1.0 - sig))).astype(BF16)
        grads[me, rows_p] = lax.dot_general(
            gpre[rows_p], w_neigh[...], (((1,), (1,)), ((), ())), preferred_element_type=F32
        ).astype(BF16)
        for i in range(N - 1):
            remote.start(gz_copy(p, i))
        remote.start(gx_copy(p, 0))
        out[rows_p] = (pre * sig).astype(BF16)
    remote.start(gc_copy(0, 0))
    stores = [pltpu.make_async_copy(out, out_h, store_sem.at[0])]
    stores[0].start()

    feat = dst.shape[1]
    pieces, wide, hid = w_full.shape
    half = pieces // 2
    for base, left in ((0, dst), (1, agg)):
        dw = lax.dot_general(left[...], gpre[...], (((0,), (0,)), ((), ())), preferred_element_type=F32)
        w_full[pl.ds(base * half, half)] = dw.reshape(half, wide, hid)
    wc_copy = remote(w_full.at[pl.ds((1 - k) * half, half)], w_c, wc_s, wc_r, sibling)
    remote.start(wc_copy)

    def from_beside(off):
        for p in range(PARTS):
            gx_copy(p, off).wait_recv()
        remote.start(gc_copy(1, off))

    for p in range(PARTS - 1):
        for i, off in enumerate(SPREAD):
            gz_copy(p, i).wait_recv()
            remote.start(gx_copy(p, off))
    wc_copy.wait_recv()
    w_half[...] = w_full[pl.ds(k * half, half)] + w_c[...]
    w_send[...] = w_half[...].astype(BF16)
    for i in range(1, 2 * N):
        remote.start(wz_copy(i))
    for i, off in enumerate(SPREAD):
        gz_copy(PARTS - 1, i).wait_recv()
        remote.start(gx_copy(PARTS - 1, off))
        remote.start(gc_copy(0, off))
        if i == 3:
            from_beside(0)

    total = w_half[x * N + z]
    for i in range(1, 2 * N):
        wz_copy(i).wait_recv()
        total += got_w[i].astype(F32)
    w_mine[...] = total
    w_rows[row] = total
    for i in range(1, 2 * N):
        remote.start(wr_copy(i))
    for off in SPREAD:
        from_beside(off)
    for i in range(2 * N):
        gc_copy(i // N, i % N).wait_recv()

    for s in range(slots):
        sums[s] = sums[table[2, s]] + lax.dot_general(
            vals[s], grads[table[5, s]], (((0,), (0,)), ((), ())), preferred_element_type=F32
        )

    def source_partial(yy, hh):
        return sums[table[3, (yy % N) * 2 + hh]]

    def h_copy(i):
        return remote(h_send.at[i], got_h.at[i], h_s.at[i], h_r.at[i], across)

    for i in range(N):
        h_send[i] = source_partial(y + OFFSETS[i], 1 - h).astype(BF16)
        remote.start(h_copy(i))

    for i in range(1, 2 * N):
        wr_copy(i).wait_recv()
    total = w_rows[0]
    for i in range(1, 2 * N):
        total += w_rows[i]
    w_out[me] = total * scale
    for i in range(1, 2 * N):
        remote.start(wg_copy(i))

    def y_copy(i):
        return remote(y_send.at[i], got_y.at[i], y_s.at[i], y_r.at[i], at_row(y + OFFSETS[i], h))

    def row_piece(i):
        own = source_partial(y + OFFSETS[i], h)
        h_copy(i).wait_recv()
        return own + got_h[i].astype(F32)

    for i in range(N - 1):
        y_send[i] = row_piece(i).astype(BF16)
        remote.start(y_copy(i))

    kept[...] = row_piece(N - 1)
    stores.append(pltpu.make_async_copy(kept, own_h, store_sem.at[1]))
    stores[1].start()
    for i in range(1, 2 * N):
        wg_copy(i).wait_recv()
    ref = pl.ds(k * half, half)
    wl_copy = remote(w_out.at[ref], w_out_h.at[ref], wl_s, wl_r, sibling)
    remote.start(wl_copy)
    stores.append(pltpu.make_async_copy(w_out.at[ref], w_out_h.at[ref], store_sem.at[2]))
    stores[2].start()
    remote.finish()
    for store in stores:
        store.wait()
    for i in range(N - 1):
        y_copy(i).wait_recv()
    wl_copy.wait_recv()


def layer(scale, rows, cols, counts, feats, vals, dst, cot, w_self, w_neigh):
    slots, block, _ = vals.shape
    width = feats.shape[-1]
    hid = w_self.shape[1]
    wide = 2 * width // (4 * N)
    results = (
        jax.ShapeDtypeStruct((block, hid), BF16),
        jax.ShapeDtypeStruct((4 * N, wide, hid), F32),
        jax.ShapeDtypeStruct((block, width), F32),
        jax.ShapeDtypeStruct((N - 1, block, width), BF16),
    )

    def like(a):
        return pltpu.VMEM(a.shape, a.dtype)

    def blocks(n, kind=BF16):
        return pltpu.VMEM((n, block, width), kind)

    def slabs(n, kind=F32):
        return pltpu.VMEM((n, wide, hid), kind)

    return pl.pallas_call(
        functools.partial(layer_kernel, scale),
        out_shape=results,
        in_specs=[HBM, HBM, SMEM] + [HBM] * 6,
        out_specs=(HBM,) * 4,
        scratch_shapes=[
            like(rows), like(cols), pltpu.VMEM((8, 128), jnp.int32), pltpu.SMEM((8, 128), jnp.int32),
            *map(like, results[:3]), like(feats), like(vals), like(dst), like(cot), like(w_self), like(w_neigh),
            blocks(slots + 1, F32), blocks(4 * N),
            blocks(2 * N), blocks(2 * N), blocks(N), blocks(N), blocks(N - 1), blocks(N - 1),
            like(dst), pltpu.VMEM(cot.shape, F32), like(cot),
            blocks(N), blocks(N), blocks(N - 1),
            slabs(4 * N), slabs(2 * N), slabs(2 * N), slabs(2 * N, BF16), slabs(2 * N, BF16),
            pltpu.VMEM((wide, hid), F32), slabs(2 * N),
            DMA((11,)), DMA, DMA((3,)),
            DMA((2 * N,)), DMA((2 * N,)), DMA((PARTS, N)), DMA((PARTS, N)), DMA((PARTS, N)), DMA((PARTS, N)),
            DMA((N,)), DMA((N,)), DMA((N,)), DMA((N,)),
            DMA((PARTS, N)), DMA((PARTS, N)), DMA((PARTS, N)), DMA((PARTS, N)), DMA((2 * N,)), DMA((2 * N,)),
            DMA, DMA, DMA((2 * N,)), DMA((2 * N,)), DMA((2 * N,)), DMA((2 * N,)), DMA((2 * N,)), DMA((2 * N,)),
            DMA, DMA,
        ],
        compiler_params=pltpu.CompilerParams(
            collective_id=0, has_side_effects=True, vmem_limit_bytes=60 * 1024 * 1024
        ),
    )(rows, cols, counts, feats, vals, dst, cot, w_self, w_neigh)


def hand_kernel(out_h, w_h, own_h, parts_h, out, w_self, w_neigh, source, out_v, w_v, own_v, parts_v, sem):
    half = w_self.shape[0]
    low, high = pl.ds(0, half), pl.ds(half, half)
    ways = (
        (parts_h, parts_v, None),
        (own_h, own_v, source),
        (w_h.at[low], w_v.at[low], w_self),
        (w_h.at[high], w_v.at[high], w_neigh),
        (out_h, out_v, out),
    )
    loads = [pltpu.make_async_copy(src, via, sem.at[0, i]) for i, (src, via, _) in enumerate(ways)]
    stores = [pltpu.make_async_copy(via, dest, sem.at[1, i]) for i, (_, via, dest) in enumerate(ways) if dest is not None]
    for load in loads:
        load.start()
    for load in loads[:2]:
        load.wait()
    total = own_v[...]
    for i in range(parts_v.shape[0]):
        total += parts_v[i].astype(F32)
    own_v[...] = total
    stores[0].start()
    for load, store in zip(loads[2:], stores[1:]):
        load.wait()
        store.start()
    for store in stores:
        store.wait()


def hand(out, w_all, own, parts):
    pieces, wide, hid = w_all.shape
    grad = jax.ShapeDtypeStruct((pieces // 2, wide, hid), F32)
    return pl.pallas_call(
        hand_kernel,
        out_shape=(jax.ShapeDtypeStruct(out.shape, BF16), grad, grad, jax.ShapeDtypeStruct(own.shape, F32)),
        in_specs=[HBM] * 4,
        out_specs=(HBM,) * 4,
        scratch_shapes=[*(pltpu.VMEM(a.shape, a.dtype) for a in (out, w_all, own, parts)), DMA((2, 5))],
        compiler_params=pltpu.CompilerParams(vmem_limit_bytes=60 * 1024 * 1024),
    )(out, w_all, own, parts)


def per_device(features, dst_features, w_self, w_neigh, cotangent, block_values, block_rows, block_cols, block_counts):
    block = block_values.shape[-1]
    width = features.shape[-1]
    nodes = dst_features.shape[0] * lax.axis_size("row") * lax.axis_size("col")
    results = layer(
        1.0 / math.sqrt(nodes), block_rows[0], block_cols[0], block_counts, features.reshape(-1, block, width),
        block_values[0, 0], dst_features, cotangent, w_self, w_neigh,
    )
    out, grad_self, grad_neigh, source = hand(*results)
    return out, grad_self.reshape(width, -1), grad_neigh.reshape(width, -1), source[None]


def solution(mesh):
    placed = (
        P("col", None, None),
        P(("row", "col"), None),
        P(),
        P(),
        P(("row", "col"), None),
        P("row", "col", None, None, None),
        P("row", "col", None),
        P("row", "col", None),
        P("row", "col"),
    )
    return jax.shard_map(
        per_device,
        mesh=mesh,
        in_specs=placed,
        out_specs=(P(("row", "col"), None), P(), P(), P("col", "row", None)),
        check_vma=False,
    )
```

```python
import functools
import math

import jax
import jax.numpy as jnp
from jax import lax
from jax.experimental import pallas as pl
from jax.experimental.pallas import tpu as pltpu
from jax.sharding import PartitionSpec as P

BF16 = jnp.bfloat16
F32 = jnp.float32
MESH = pl.DeviceIdType.MESH
N = 8
SHARES = (64, 64)
PARTS = len(SHARES)
OFFSETS = (4, 3, 5, 2, 6, 1, 7, 0)
GREETED = (12, 4, 11, 13, 3, 5, 10, 14, 2, 6, 9, 15, 1, 7, 8)
SPREAD = (4, 3, 5, 2, 6, 1, 7)
SMEM = pl.BlockSpec(memory_space=pltpu.SMEM)
HBM = pl.BlockSpec(memory_space=pltpu.HBM)
DMA = pltpu.SemaphoreType.DMA


class Copies:
    def __init__(self):
        self.started = []

    def __call__(self, src, dst, send, recv, device):
        return pltpu.make_async_remote_copy(
            src_ref=src, dst_ref=dst, send_sem=send, recv_sem=recv, device_id=device, device_id_type=MESH
        )

    def start(self, copy):
        copy.start()
        self.started.append(copy)

    def finish(self):
        for copy in self.started:
            copy.wait_send()
        self.started = []


def chain(ids, live):
    slots = ids.shape[1]
    t = lax.broadcasted_iota(jnp.int32, (slots, slots), 0)
    s = lax.broadcasted_iota(jnp.int32, (slots, slots), 1)
    along = jnp.broadcast_to(ids, (slots, slots))
    down = jnp.sum(jnp.where(t == s, along, 0), axis=1, keepdims=True)
    used = t < live
    prev = jnp.max(jnp.where((down == along) & (t < s) & used, t, -1), axis=0, keepdims=True)
    last = jnp.max(jnp.where((down == s) & used, t, -1), axis=0, keepdims=True)
    return jnp.where(prev < 0, slots, prev), jnp.where(last < 0, slots, last)


def layer_kernel(
    scale,
    rows_h, cols_h, counts, feats_h, vals_h, dst_h, cot_h, w_self_h, w_neigh_h,
    out_h, w_out_h, own_h, got_y,
    rows, cols, tables, table, out, w_out, kept, feats, vals, dst, cot, w_self, w_neigh, sums, grads,
    c_send, got_c, x_send, got_x, z_send, got_z, agg, pre_self, gpre,
    h_send, got_h, y_send,
    w_full, w_c, w_half, w_send, got_w, w_mine, w_rows,
    load_sem, table_sem, store_sem,
    c_s, c_r, x_s, x_r, z_s, z_r, h_s, h_r, y_s, y_r,
    gz_s, gz_r, gx_s, gx_r, gc_s, gc_r,
    wc_s, wc_r, wz_s, wz_r, wr_s, wr_r, wg_s, wg_r, wl_s, wl_r,
):
    remote = Copies()
    row, col = lax.axis_index("row"), lax.axis_index("col")
    z, x, k = col // 4, (col // 2) % 2, col % 2
    y, h = row // 2, row % 2
    slots = vals.shape[0]
    quarter = slots // 4
    shares = [pl.ds(sum(SHARES[:p]), tall) for p, tall in enumerate(SHARES)]

    def at_col(zz, xx, kk):
        return (row, (zz % N) * 4 + xx * 2 + kk)

    def at_row(yy, hh):
        return ((yy % N) * 2 + hh, col)

    mine = k * 2 * N + x * N
    me = mine + z
    sibling, beside, across = at_col(z, x, 1 - k), at_col(z, 1 - x, k), at_row(y, 1 - h)

    def near(i):
        return at_col(z + i % N, (x + i // N) % 2, k)

    def far(i):
        return at_row(y + i % N, (h + i // N) % 2)

    def wz_copy(i):
        ref = w_send.at[((x + i // N) % 2) * N + (z + i) % N]
        return remote(ref, got_w.at[i], wz_s.at[i], wz_r.at[i], near(i))

    def wr_copy(i):
        return remote(w_mine, w_rows.at[row], wr_s.at[i], wr_r.at[i], far(i))

    def wg_copy(i):
        return remote(w_out.at[me], w_out.at[me], wg_s.at[i], wg_r.at[i], near(i))

    barrier = pltpu.get_barrier_semaphore()

    def greet(device):
        pl.semaphore_signal(barrier, inc=1, device_id=device, device_id_type=MESH)

    for i in GREETED:
        greet(far(i))
        greet(near(i))
    greet(sibling)

    loads = []
    for i, (src, dest) in enumerate(((rows_h, rows), (cols_h, cols), (feats_h, feats))):
        loads.append(pltpu.make_async_copy(src, dest, load_sem.at[i]))
    for i in range(4):
        part = pl.ds(i * quarter, quarter)
        loads.append(pltpu.make_async_copy(vals_h.at[part], vals.at[part], load_sem.at[3 + i]))
    for i, (src, dest) in enumerate(((dst_h, dst), (w_self_h, w_self), (w_neigh_h, w_neigh), (cot_h, cot))):
        loads.append(pltpu.make_async_copy(src, dest, load_sem.at[7 + i]))
    for load in loads:
        load.start()

    sums[slots] = jnp.zeros_like(sums[slots])
    tables[...] = jnp.zeros_like(tables)
    for load in loads[:2]:
        load.wait()
    r, c = rows[...], cols[...]
    row_prev, row_last = chain(r, counts[0, 0])
    col_prev, col_last = chain(c, counts[0, 0])
    at = (r % 2) * (2 * N) + ((r // 2) % 2) * N + r // 4
    for i, line in enumerate((row_prev, row_last, col_prev, col_last, c, at)):
        tables[pl.ds(i, 1), pl.ds(0, slots)] = line
    to_scalars = pltpu.make_async_copy(tables, table, table_sem)
    to_scalars.start()
    to_scalars.wait()

    loads[2].wait()
    for s in range(slots):
        if s % quarter == 0:
            loads[3 + s // quarter].wait()
        sums[s] = sums[table[0, s]] + jnp.dot(vals[s], feats[table[4, s]], preferred_element_type=F32)

    def partial(zz, xx, kk):
        return sums[table[1, (zz % N) * 4 + xx * 2 + kk]]

    for i in range(2 * N):
        c_send[i] = partial(z + OFFSETS[i % N], 1 - x if i < N else x, 1 - k).astype(BF16)
    for load in loads[7:]:
        load.wait()
    pre_self[...] = jnp.dot(dst[...], w_self[...], preferred_element_type=F32)
    pl.semaphore_wait(barrier, 4 * N - 1)

    def c_copy(i):
        return remote(c_send.at[i], got_c.at[i], c_s.at[i], c_r.at[i], sibling)

    for i in range(N):
        remote.start(c_copy(i))

    def x_copy(p, i):
        return remote(
            x_send.at[i, shares[p]], got_x.at[i, shares[p]], x_s.at[p, i], x_r.at[p, i], beside
        )

    for i in range(N):
        own = partial(z + OFFSETS[i], 1 - x, k)
        c_copy(i).wait_recv()
        x_send[i] = (own + got_c[i].astype(F32)).astype(BF16)
        remote.start(x_copy(0, i))
        remote.start(c_copy(N + i))
    for p in range(1, PARTS):
        for i in range(N):
            remote.start(x_copy(p, i))

    def col_piece(p, i):
        first = sum(SHARES[:p])
        own = partial(z + OFFSETS[i], x, k)[first : first + SHARES[p]]
        if p == 0:
            c_copy(N + i).wait_recv()
        own += got_c[N + i, shares[p]].astype(F32)
        x_copy(p, i).wait_recv()
        return own + got_x[i, shares[p]].astype(F32)

    def z_copy(p, i):
        return remote(
            z_send.at[i, shares[p]], got_z.at[i, shares[p]], z_s.at[p, i], z_r.at[p, i], at_col(z + OFFSETS[i], x, k)
        )

    def gz_copy(p, i):
        ref = grads.at[me, shares[p]]
        return remote(ref, ref, gz_s.at[p, i], gz_r.at[p, i], at_col(z + SPREAD[i], x, k))

    def gx_copy(p, off):
        ref = grads.at[mine + (z + N - off) % N, shares[p]]
        return remote(ref, ref, gx_s.at[p, off], gx_r.at[p, off], beside)

    def gc_copy(other, off):
        ref = grads.at[k * 2 * N + ((x + other) % 2) * N + (z + N - off) % N]
        return remote(ref, ref, gc_s.at[other * N + off], gc_r.at[other * N + off], sibling)

    totals = []
    for p in range(PARTS):
        for i in range(N - 1):
            z_send[i, shares[p]] = col_piece(p, i).astype(BF16)
            remote.start(z_copy(p, i))
        totals.append(col_piece(p, N - 1))

    for p, rows_p in enumerate(shares):
        total = totals[p]
        for i in range(N - 1):
            z_copy(p, i).wait_recv()
            total += got_z[i, rows_p].astype(F32)
        agg[rows_p] = total.astype(BF16)
        pre = pre_self[rows_p] + jnp.dot(agg[rows_p], w_neigh[...], preferred_element_type=F32)
        sig = jax.nn.sigmoid(pre)
        gpre[rows_p] = (cot[rows_p].astype(F32) * sig * (1.0 + pre * (1.0 - sig))).astype(BF16)
        grads[me, rows_p] = lax.dot_general(
            gpre[rows_p], w_neigh[...], (((1,), (1,)), ((), ())), preferred_element_type=F32
        ).astype(BF16)
        for i in range(N - 1):
            remote.start(gz_copy(p, i))
        remote.start(gx_copy(p, 0))
        out[rows_p] = (pre * sig).astype(BF16)
    remote.start(gc_copy(0, 0))
    stores = [pltpu.make_async_copy(out, out_h, store_sem.at[0])]
    stores[0].start()

    feat = dst.shape[1]
    pieces, wide, hid = w_full.shape
    half = pieces // 2
    for base, left in ((0, dst), (1, agg)):
        dw = lax.dot_general(left[...], gpre[...], (((0,), (0,)), ((), ())), preferred_element_type=F32)
        w_full[pl.ds(base * half, half)] = dw.reshape(half, wide, hid)
    wc_copy = remote(w_full.at[pl.ds((1 - k) * half, half)], w_c, wc_s, wc_r, sibling)
    remote.start(wc_copy)

    def from_beside(off):
        for p in range(PARTS):
            gx_copy(p, off).wait_recv()
        remote.start(gc_copy(1, off))

    for p in range(PARTS - 1):
        for i, off in enumerate(SPREAD):
            gz_copy(p, i).wait_recv()
            remote.start(gx_copy(p, off))
    wc_copy.wait_recv()
    w_half[...] = w_full[pl.ds(k * half, half)] + w_c[...]
    w_send[...] = w_half[...].astype(BF16)
    for i in range(1, 2 * N):
        remote.start(wz_copy(i))
    for i, off in enumerate(SPREAD):
        gz_copy(PARTS - 1, i).wait_recv()
        remote.start(gx_copy(PARTS - 1, off))
        remote.start(gc_copy(0, off))
        if i == 3:
            from_beside(0)

    total = w_half[x * N + z]
    for i in range(1, 2 * N):
        wz_copy(i).wait_recv()
        total += got_w[i].astype(F32)
    w_mine[...] = total
    w_rows[row] = total
    for i in range(1, 2 * N):
        remote.start(wr_copy(i))
    for off in SPREAD:
        from_beside(off)
    for i in range(2 * N):
        gc_copy(i // N, i % N).wait_recv()

    for s in range(slots):
        sums[s] = sums[table[2, s]] + lax.dot_general(
            vals[s], grads[table[5, s]], (((0,), (0,)), ((), ())), preferred_element_type=F32
        )

    def source_partial(yy, hh):
        return sums[table[3, (yy % N) * 2 + hh]]

    def h_copy(i):
        return remote(h_send.at[i], got_h.at[i], h_s.at[i], h_r.at[i], across)

    for i in range(N):
        h_send[i] = source_partial(y + OFFSETS[i], 1 - h).astype(BF16)
        remote.start(h_copy(i))

    for i in range(1, 2 * N):
        wr_copy(i).wait_recv()
    total = w_rows[0]
    for i in range(1, 2 * N):
        total += w_rows[i]
    w_out[me] = total * scale
    for i in range(1, 2 * N):
        remote.start(wg_copy(i))

    def y_copy(i):
        return remote(y_send.at[i], got_y.at[i], y_s.at[i], y_r.at[i], at_row(y + OFFSETS[i], h))

    def row_piece(i):
        own = source_partial(y + OFFSETS[i], h)
        h_copy(i).wait_recv()
        return own + got_h[i].astype(F32)

    for i in range(N - 1):
        y_send[i] = row_piece(i).astype(BF16)
        remote.start(y_copy(i))

    kept[...] = row_piece(N - 1)
    stores.append(pltpu.make_async_copy(kept, own_h, store_sem.at[1]))
    stores[1].start()
    for i in range(1, 2 * N):
        wg_copy(i).wait_recv()
    ref = pl.ds(k * half, half)
    wl_copy = remote(w_out.at[ref], w_out_h.at[ref], wl_s, wl_r, sibling)
    remote.start(wl_copy)
    stores.append(pltpu.make_async_copy(w_out.at[ref], w_out_h.at[ref], store_sem.at[2]))
    stores[2].start()
    remote.finish()
    for store in stores:
        store.wait()
    for i in range(N - 1):
        y_copy(i).wait_recv()
    wl_copy.wait_recv()


def layer(scale, rows, cols, counts, feats, vals, dst, cot, w_self, w_neigh):
    slots, block, _ = vals.shape
    width = feats.shape[-1]
    hid = w_self.shape[1]
    wide = 2 * width // (4 * N)
    results = (
        jax.ShapeDtypeStruct((block, hid), BF16),
        jax.ShapeDtypeStruct((4 * N, wide, hid), F32),
        jax.ShapeDtypeStruct((block, width), F32),
        jax.ShapeDtypeStruct((N - 1, block, width), BF16),
    )

    def like(a):
        return pltpu.VMEM(a.shape, a.dtype)

    def blocks(n, kind=BF16):
        return pltpu.VMEM((n, block, width), kind)

    def slabs(n, kind=F32):
        return pltpu.VMEM((n, wide, hid), kind)

    return pl.pallas_call(
        functools.partial(layer_kernel, scale),
        out_shape=results,
        in_specs=[HBM, HBM, SMEM] + [HBM] * 6,
        out_specs=(HBM,) * 4,
        scratch_shapes=[
            like(rows), like(cols), pltpu.VMEM((8, 128), jnp.int32), pltpu.SMEM((8, 128), jnp.int32),
            *map(like, results[:3]), like(feats), like(vals), like(dst), like(cot), like(w_self), like(w_neigh),
            blocks(slots + 1, F32), blocks(4 * N),
            blocks(2 * N), blocks(2 * N), blocks(N), blocks(N), blocks(N - 1), blocks(N - 1),
            like(dst), pltpu.VMEM(cot.shape, F32), like(cot),
            blocks(N), blocks(N), blocks(N - 1),
            slabs(4 * N), slabs(2 * N), slabs(2 * N), slabs(2 * N, BF16), slabs(2 * N, BF16),
            pltpu.VMEM((wide, hid), F32), slabs(2 * N),
            DMA((11,)), DMA, DMA((3,)),
            DMA((2 * N,)), DMA((2 * N,)), DMA((PARTS, N)), DMA((PARTS, N)), DMA((PARTS, N)), DMA((PARTS, N)),
            DMA((N,)), DMA((N,)), DMA((N,)), DMA((N,)),
            DMA((PARTS, N)), DMA((PARTS, N)), DMA((PARTS, N)), DMA((PARTS, N)), DMA((2 * N,)), DMA((2 * N,)),
            DMA, DMA, DMA((2 * N,)), DMA((2 * N,)), DMA((2 * N,)), DMA((2 * N,)), DMA((2 * N,)), DMA((2 * N,)),
            DMA, DMA,
        ],
        compiler_params=pltpu.CompilerParams(
            collective_id=0, has_side_effects=True, vmem_limit_bytes=60 * 1024 * 1024
        ),
    )(rows, cols, counts, feats, vals, dst, cot, w_self, w_neigh)


def hand_kernel(out_h, w_h, own_h, parts_h, out, w_self, w_neigh, source, out_v, w_v, own_v, parts_v, sem):
    half = w_self.shape[0]
    low, high = pl.ds(0, half), pl.ds(half, half)
    ways = (
        (parts_h, parts_v, None),
        (own_h, own_v, source),
        (w_h.at[low], w_v.at[low], w_self),
        (w_h.at[high], w_v.at[high], w_neigh),
        (out_h, out_v, out),
    )
    loads = [pltpu.make_async_copy(src, via, sem.at[0, i]) for i, (src, via, _) in enumerate(ways)]
    stores = [pltpu.make_async_copy(via, dest, sem.at[1, i]) for i, (_, via, dest) in enumerate(ways) if dest is not None]
    for load in loads:
        load.start()
    for load in loads[:2]:
        load.wait()
    total = own_v[...]
    for i in range(parts_v.shape[0]):
        total += parts_v[i].astype(F32)
    own_v[...] = total
    stores[0].start()
    for load, store in zip(loads[2:], stores[1:]):
        load.wait()
        store.start()
    for store in stores:
        store.wait()


def hand(out, w_all, own, parts):
    pieces, wide, hid = w_all.shape
    grad = jax.ShapeDtypeStruct((pieces // 2, wide, hid), F32)
    return pl.pallas_call(
        hand_kernel,
        out_shape=(jax.ShapeDtypeStruct(out.shape, BF16), grad, grad, jax.ShapeDtypeStruct(own.shape, F32)),
        in_specs=[HBM] * 4,
        out_specs=(HBM,) * 4,
        scratch_shapes=[*(pltpu.VMEM(a.shape, a.dtype) for a in (out, w_all, own, parts)), DMA((2, 5))],
        compiler_params=pltpu.CompilerParams(vmem_limit_bytes=60 * 1024 * 1024),
    )(out, w_all, own, parts)


def per_device(features, dst_features, w_self, w_neigh, cotangent, block_values, block_rows, block_cols, block_counts):
    block = block_values.shape[-1]
    width = features.shape[-1]
    nodes = dst_features.shape[0] * lax.axis_size("row") * lax.axis_size("col")
    results = layer(
        1.0 / math.sqrt(nodes), block_rows[0], block_cols[0], block_counts, features.reshape(-1, block, width),
        block_values[0, 0], dst_features, cotangent, w_self, w_neigh,
    )
    out, grad_self, grad_neigh, source = hand(*results)
    return out, grad_self.reshape(width, -1), grad_neigh.reshape(width, -1), source[None]


def solution(mesh):
    placed = (
        P("col", None, None),
        P(("row", "col"), None),
        P(),
        P(),
        P(("row", "col"), None),
        P("row", "col", None, None, None),
        P("row", "col", None),
        P("row", "col", None),
        P("row", "col"),
    )
    return jax.shard_map(
        per_device,
        mesh=mesh,
        in_specs=placed,
        out_specs=(P(("row", "col"), None), P(), P(), P("col", "row", None)),
        check_vma=False,
    )
```

```python
import functools
import math

import jax
import jax.numpy as jnp
from jax import lax
from jax.experimental import pallas as pl
from jax.experimental.pallas import tpu as pltpu
from jax.sharding import PartitionSpec as P

BF16 = jnp.bfloat16
F32 = jnp.float32
MESH = pl.DeviceIdType.MESH
N = 8
SHARES = (64, 64)
PARTS = len(SHARES)
OFFSETS = (4, 3, 5, 2, 6, 1, 7, 0)
GREETED = (12, 4, 11, 13, 3, 5, 10, 14, 2, 6, 9, 15, 1, 7, 8)
SPREAD = (4, 3, 5, 2, 6, 1, 7)
SMEM = pl.BlockSpec(memory_space=pltpu.SMEM)
HBM = pl.BlockSpec(memory_space=pltpu.HBM)
DMA = pltpu.SemaphoreType.DMA


class Copies:
    def __init__(self):
        self.started = []

    def __call__(self, src, dst, send, recv, device):
        return pltpu.make_async_remote_copy(
            src_ref=src, dst_ref=dst, send_sem=send, recv_sem=recv, device_id=device, device_id_type=MESH
        )

    def start(self, copy):
        copy.start()
        self.started.append(copy)

    def finish(self):
        for copy in self.started:
            copy.wait_send()
        self.started = []


def chain(ids, live):
    slots = ids.shape[1]
    t = lax.broadcasted_iota(jnp.int32, (slots, slots), 0)
    s = lax.broadcasted_iota(jnp.int32, (slots, slots), 1)
    along = jnp.broadcast_to(ids, (slots, slots))
    down = jnp.sum(jnp.where(t == s, along, 0), axis=1, keepdims=True)
    used = t < live
    prev = jnp.max(jnp.where((down == along) & (t < s) & used, t, -1), axis=0, keepdims=True)
    last = jnp.max(jnp.where((down == s) & used, t, -1), axis=0, keepdims=True)
    return jnp.where(prev < 0, slots, prev), jnp.where(last < 0, slots, last)


def layer_kernel(
    scale,
    rows_h, cols_h, counts, feats_h, vals_h, dst_h, cot_h, w_self_h, w_neigh_h,
    out_h, w_out_h, own_h, got_y,
    rows, cols, tables, table, out, w_out, kept, feats, vals, dst, cot, w_self, w_neigh, sums, grads,
    c_send, got_c, x_send, got_x, z_send, got_z, agg, pre_self, gpre,
    h_send, got_h, y_send,
    w_full, w_c, w_half, w_send, got_w, w_mine, w_rows,
    load_sem, table_sem, store_sem,
    c_s, c_r, x_s, x_r, z_s, z_r, h_s, h_r, y_s, y_r,
    gz_s, gz_r, gx_s, gx_r, gc_s, gc_r,
    wc_s, wc_r, wz_s, wz_r, wr_s, wr_r, wg_s, wg_r, wl_s, wl_r,
):
    remote = Copies()
    row, col = lax.axis_index("row"), lax.axis_index("col")
    z, x, k = col // 4, (col // 2) % 2, col % 2
    y, h = row // 2, row % 2
    slots = vals.shape[0]
    quarter = slots // 4
    shares = [pl.ds(sum(SHARES[:p]), tall) for p, tall in enumerate(SHARES)]

    def at_col(zz, xx, kk):
        return (row, (zz % N) * 4 + xx * 2 + kk)

    def at_row(yy, hh):
        return ((yy % N) * 2 + hh, col)

    mine = k * 2 * N + x * N
    me = mine + z
    sibling, beside, across = at_col(z, x, 1 - k), at_col(z, 1 - x, k), at_row(y, 1 - h)

    def near(i):
        return at_col(z + i % N, (x + i // N) % 2, k)

    def far(i):
        return at_row(y + i % N, (h + i // N) % 2)

    def wz_copy(i):
        ref = w_send.at[((x + i // N) % 2) * N + (z + i) % N]
        return remote(ref, got_w.at[i], wz_s.at[i], wz_r.at[i], near(i))

    def wr_copy(i):
        return remote(w_mine, w_rows.at[row], wr_s.at[i], wr_r.at[i], far(i))

    def wg_copy(i):
        return remote(w_out.at[me], w_out.at[me], wg_s.at[i], wg_r.at[i], near(i))

    barrier = pltpu.get_barrier_semaphore()

    def greet(device):
        pl.semaphore_signal(barrier, inc=1, device_id=device, device_id_type=MESH)

    for i in GREETED:
        greet(far(i))
        greet(near(i))
    greet(sibling)

    loads = []
    for i, (src, dest) in enumerate(((rows_h, rows), (cols_h, cols), (feats_h, feats))):
        loads.append(pltpu.make_async_copy(src, dest, load_sem.at[i]))
    for i in range(4):
        part = pl.ds(i * quarter, quarter)
        loads.append(pltpu.make_async_copy(vals_h.at[part], vals.at[part], load_sem.at[3 + i]))
    for i, (src, dest) in enumerate(((dst_h, dst), (w_self_h, w_self), (w_neigh_h, w_neigh), (cot_h, cot))):
        loads.append(pltpu.make_async_copy(src, dest, load_sem.at[7 + i]))
    for load in loads:
        load.start()

    sums[slots] = jnp.zeros_like(sums[slots])
    tables[...] = jnp.zeros_like(tables)
    for load in loads[:2]:
        load.wait()
    r, c = rows[...], cols[...]
    row_prev, row_last = chain(r, counts[0, 0])
    col_prev, col_last = chain(c, counts[0, 0])
    at = (r % 2) * (2 * N) + ((r // 2) % 2) * N + r // 4
    for i, line in enumerate((row_prev, row_last, col_prev, col_last, c, at)):
        tables[pl.ds(i, 1), pl.ds(0, slots)] = line
    to_scalars = pltpu.make_async_copy(tables, table, table_sem)
    to_scalars.start()
    to_scalars.wait()

    loads[2].wait()
    for s in range(slots):
        if s % quarter == 0:
            loads[3 + s // quarter].wait()
        sums[s] = sums[table[0, s]] + jnp.dot(vals[s], feats[table[4, s]], preferred_element_type=F32)

    def partial(zz, xx, kk):
        return sums[table[1, (zz % N) * 4 + xx * 2 + kk]]

    for i in range(2 * N):
        c_send[i] = partial(z + OFFSETS[i % N], 1 - x if i < N else x, 1 - k).astype(BF16)
    for load in loads[7:]:
        load.wait()
    pre_self[...] = jnp.dot(dst[...], w_self[...], preferred_element_type=F32)
    pl.semaphore_wait(barrier, 4 * N - 1)

    def c_copy(i):
        return remote(c_send.at[i], got_c.at[i], c_s.at[i], c_r.at[i], sibling)

    for i in range(N):
        remote.start(c_copy(i))

    def x_copy(p, i):
        return remote(
            x_send.at[i, shares[p]], got_x.at[i, shares[p]], x_s.at[p, i], x_r.at[p, i], beside
        )

    for i in range(N):
        own = partial(z + OFFSETS[i], 1 - x, k)
        c_copy(i).wait_recv()
        x_send[i] = (own + got_c[i].astype(F32)).astype(BF16)
        remote.start(x_copy(0, i))
        remote.start(c_copy(N + i))
    for p in range(1, PARTS):
        for i in range(N):
            remote.start(x_copy(p, i))

    def col_piece(p, i):
        first = sum(SHARES[:p])
        own = partial(z + OFFSETS[i], x, k)[first : first + SHARES[p]]
        if p == 0:
            c_copy(N + i).wait_recv()
        own += got_c[N + i, shares[p]].astype(F32)
        x_copy(p, i).wait_recv()
        return own + got_x[i, shares[p]].astype(F32)

    def z_copy(p, i):
        return remote(
            z_send.at[i, shares[p]], got_z.at[i, shares[p]], z_s.at[p, i], z_r.at[p, i], at_col(z + OFFSETS[i], x, k)
        )

    def gz_copy(p, i):
        ref = grads.at[me, shares[p]]
        return remote(ref, ref, gz_s.at[p, i], gz_r.at[p, i], at_col(z + SPREAD[i], x, k))

    def gx_copy(p, off):
        ref = grads.at[mine + (z + N - off) % N, shares[p]]
        return remote(ref, ref, gx_s.at[p, off], gx_r.at[p, off], beside)

    def gc_copy(other, off):
        ref = grads.at[k * 2 * N + ((x + other) % 2) * N + (z + N - off) % N]
        return remote(ref, ref, gc_s.at[other * N + off], gc_r.at[other * N + off], sibling)

    totals = []
    for p in range(PARTS):
        for i in range(N - 1):
            z_send[i, shares[p]] = col_piece(p, i).astype(BF16)
            remote.start(z_copy(p, i))
        totals.append(col_piece(p, N - 1))

    for p, rows_p in enumerate(shares):
        total = totals[p]
        for i in range(N - 1):
            z_copy(p, i).wait_recv()
            total += got_z[i, rows_p].astype(F32)
        agg[rows_p] = total.astype(BF16)
        pre = pre_self[rows_p] + jnp.dot(agg[rows_p], w_neigh[...], preferred_element_type=F32)
        sig = jax.nn.sigmoid(pre)
        gpre[rows_p] = (cot[rows_p].astype(F32) * sig * (1.0 + pre * (1.0 - sig))).astype(BF16)
        grads[me, rows_p] = lax.dot_general(
            gpre[rows_p], w_neigh[...], (((1,), (1,)), ((), ())), preferred_element_type=F32
        ).astype(BF16)
        for i in range(N - 1):
            remote.start(gz_copy(p, i))
        remote.start(gx_copy(p, 0))
        out[rows_p] = (pre * sig).astype(BF16)
    remote.start(gc_copy(0, 0))
    stores = [pltpu.make_async_copy(out, out_h, store_sem.at[0])]
    stores[0].start()

    feat = dst.shape[1]
    pieces, wide, hid = w_full.shape
    half = pieces // 2
    for base, left in ((0, dst), (1, agg)):
        dw = lax.dot_general(left[...], gpre[...], (((0,), (0,)), ((), ())), preferred_element_type=F32)
        w_full[pl.ds(base * half, half)] = dw.reshape(half, wide, hid)
    wc_copy = remote(w_full.at[pl.ds((1 - k) * half, half)], w_c, wc_s, wc_r, sibling)
    remote.start(wc_copy)

    def from_beside(off):
        for p in range(PARTS):
            gx_copy(p, off).wait_recv()
        remote.start(gc_copy(1, off))

    for p in range(PARTS - 1):
        for i, off in enumerate(SPREAD):
            gz_copy(p, i).wait_recv()
            remote.start(gx_copy(p, off))
    wc_copy.wait_recv()
    w_half[...] = w_full[pl.ds(k * half, half)] + w_c[...]
    w_send[...] = w_half[...].astype(BF16)
    for i in range(1, 2 * N):
        remote.start(wz_copy(i))
    for i, off in enumerate(SPREAD):
        gz_copy(PARTS - 1, i).wait_recv()
        remote.start(gx_copy(PARTS - 1, off))
        remote.start(gc_copy(0, off))

    total = w_half[x * N + z]
    for i in range(1, 2 * N):
        wz_copy(i).wait_recv()
        total += got_w[i].astype(F32)
    w_mine[...] = total
    w_rows[row] = total
    for i in range(1, 2 * N):
        remote.start(wr_copy(i))
    for off in (0, *SPREAD):
        from_beside(off)
    for i in range(2 * N):
        gc_copy(i // N, i % N).wait_recv()

    for s in range(slots):
        sums[s] = sums[table[2, s]] + lax.dot_general(
            vals[s], grads[table[5, s]], (((0,), (0,)), ((), ())), preferred_element_type=F32
        )

    def source_partial(yy, hh):
        return sums[table[3, (yy % N) * 2 + hh]]

    def h_copy(i):
        return remote(h_send.at[i], got_h.at[i], h_s.at[i], h_r.at[i], across)

    for i in range(N):
        h_send[i] = source_partial(y + OFFSETS[i], 1 - h).astype(BF16)
        remote.start(h_copy(i))

    def y_copy(i):
        return remote(y_send.at[i], got_y.at[i], y_s.at[i], y_r.at[i], at_row(y + OFFSETS[i], h))

    def row_piece(i):
        own = source_partial(y + OFFSETS[i], h)
        h_copy(i).wait_recv()
        return own + got_h[i].astype(F32)

    def row_sum():
        for i in range(1, 2 * N):
            wr_copy(i).wait_recv()
        total = w_rows[0]
        for i in range(1, 2 * N):
            total += w_rows[i]
        w_out[me] = total * scale
        for i in range(1, 2 * N):
            remote.start(wg_copy(i))

    for i in range(N - 1):
        if i == 2:
            row_sum()
        y_send[i] = row_piece(i).astype(BF16)
        remote.start(y_copy(i))

    kept[...] = row_piece(N - 1)
    stores.append(pltpu.make_async_copy(kept, own_h, store_sem.at[1]))
    stores[1].start()
    for i in range(1, 2 * N):
        wg_copy(i).wait_recv()
    ref = pl.ds(k * half, half)
    wl_copy = remote(w_out.at[ref], w_out_h.at[ref], wl_s, wl_r, sibling)
    remote.start(wl_copy)
    stores.append(pltpu.make_async_copy(w_out.at[ref], w_out_h.at[ref], store_sem.at[2]))
    stores[2].start()
    remote.finish()
    for store in stores:
        store.wait()
    for i in range(N - 1):
        y_copy(i).wait_recv()
    wl_copy.wait_recv()


def layer(scale, rows, cols, counts, feats, vals, dst, cot, w_self, w_neigh):
    slots, block, _ = vals.shape
    width = feats.shape[-1]
    hid = w_self.shape[1]
    wide = 2 * width // (4 * N)
    results = (
        jax.ShapeDtypeStruct((block, hid), BF16),
        jax.ShapeDtypeStruct((4 * N, wide, hid), F32),
        jax.ShapeDtypeStruct((block, width), F32),
        jax.ShapeDtypeStruct((N - 1, block, width), BF16),
    )

    def like(a):
        return pltpu.VMEM(a.shape, a.dtype)

    def blocks(n, kind=BF16):
        return pltpu.VMEM((n, block, width), kind)

    def slabs(n, kind=F32):
        return pltpu.VMEM((n, wide, hid), kind)

    return pl.pallas_call(
        functools.partial(layer_kernel, scale),
        out_shape=results,
        in_specs=[HBM, HBM, SMEM] + [HBM] * 6,
        out_specs=(HBM,) * 4,
        scratch_shapes=[
            like(rows), like(cols), pltpu.VMEM((8, 128), jnp.int32), pltpu.SMEM((8, 128), jnp.int32),
            *map(like, results[:3]), like(feats), like(vals), like(dst), like(cot), like(w_self), like(w_neigh),
            blocks(slots + 1, F32), blocks(4 * N),
            blocks(2 * N), blocks(2 * N), blocks(N), blocks(N), blocks(N - 1), blocks(N - 1),
            like(dst), pltpu.VMEM(cot.shape, F32), like(cot),
            blocks(N), blocks(N), blocks(N - 1),
            slabs(4 * N), slabs(2 * N), slabs(2 * N), slabs(2 * N, BF16), slabs(2 * N, BF16),
            pltpu.VMEM((wide, hid), F32), slabs(2 * N),
            DMA((11,)), DMA, DMA((3,)),
            DMA((2 * N,)), DMA((2 * N,)), DMA((PARTS, N)), DMA((PARTS, N)), DMA((PARTS, N)), DMA((PARTS, N)),
            DMA((N,)), DMA((N,)), DMA((N,)), DMA((N,)),
            DMA((PARTS, N)), DMA((PARTS, N)), DMA((PARTS, N)), DMA((PARTS, N)), DMA((2 * N,)), DMA((2 * N,)),
            DMA, DMA, DMA((2 * N,)), DMA((2 * N,)), DMA((2 * N,)), DMA((2 * N,)), DMA((2 * N,)), DMA((2 * N,)),
            DMA, DMA,
        ],
        compiler_params=pltpu.CompilerParams(
            collective_id=0, has_side_effects=True, vmem_limit_bytes=60 * 1024 * 1024
        ),
    )(rows, cols, counts, feats, vals, dst, cot, w_self, w_neigh)


def hand_kernel(out_h, w_h, own_h, parts_h, out, w_self, w_neigh, source, out_v, w_v, own_v, parts_v, sem):
    half = w_self.shape[0]
    low, high = pl.ds(0, half), pl.ds(half, half)
    ways = (
        (parts_h, parts_v, None),
        (own_h, own_v, source),
        (w_h.at[low], w_v.at[low], w_self),
        (w_h.at[high], w_v.at[high], w_neigh),
        (out_h, out_v, out),
    )
    loads = [pltpu.make_async_copy(src, via, sem.at[0, i]) for i, (src, via, _) in enumerate(ways)]
    stores = [pltpu.make_async_copy(via, dest, sem.at[1, i]) for i, (_, via, dest) in enumerate(ways) if dest is not None]
    for load in loads:
        load.start()
    for load in loads[:2]:
        load.wait()
    total = own_v[...]
    for i in range(parts_v.shape[0]):
        total += parts_v[i].astype(F32)
    own_v[...] = total
    stores[0].start()
    for load, store in zip(loads[2:], stores[1:]):
        load.wait()
        store.start()
    for store in stores:
        store.wait()


def hand(out, w_all, own, parts):
    pieces, wide, hid = w_all.shape
    grad = jax.ShapeDtypeStruct((pieces // 2, wide, hid), F32)
    return pl.pallas_call(
        hand_kernel,
        out_shape=(jax.ShapeDtypeStruct(out.shape, BF16), grad, grad, jax.ShapeDtypeStruct(own.shape, F32)),
        in_specs=[HBM] * 4,
        out_specs=(HBM,) * 4,
        scratch_shapes=[*(pltpu.VMEM(a.shape, a.dtype) for a in (out, w_all, own, parts)), DMA((2, 5))],
        compiler_params=pltpu.CompilerParams(vmem_limit_bytes=60 * 1024 * 1024),
    )(out, w_all, own, parts)


def per_device(features, dst_features, w_self, w_neigh, cotangent, block_values, block_rows, block_cols, block_counts):
    block = block_values.shape[-1]
    width = features.shape[-1]
    nodes = dst_features.shape[0] * lax.axis_size("row") * lax.axis_size("col")
    results = layer(
        1.0 / math.sqrt(nodes), block_rows[0], block_cols[0], block_counts, features.reshape(-1, block, width),
        block_values[0, 0], dst_features, cotangent, w_self, w_neigh,
    )
    out, grad_self, grad_neigh, source = hand(*results)
    return out, grad_self.reshape(width, -1), grad_neigh.reshape(width, -1), source[None]


def solution(mesh):
    placed = (
        P("col", None, None),
        P(("row", "col"), None),
        P(),
        P(),
        P(("row", "col"), None),
        P("row", "col", None, None, None),
        P("row", "col", None),
        P("row", "col", None),
        P("row", "col"),
    )
    return jax.shard_map(
        per_device,
        mesh=mesh,
        in_specs=placed,
        out_specs=(P(("row", "col"), None), P(), P(), P("col", "row", None)),
        check_vma=False,
    )
```
